32 devices in a mesh: ctx: 8 (over z, y), tp: 4 (over x, core).
Axes of the slice: x: 2, y: 2, z: 4, core: 2. Of those that a mesh axis runs over, the one named last changes fastest.
Arguments:
- queries: bfloat16 [2048, 8192], P('ctx', 'tp'), may hold values from -8 to 8
- keys: bfloat16 [2048, 1024], P('ctx', 'tp'), may hold values from -8 to 8
- values: bfloat16 [2048, 1024], P('ctx', 'tp'), may hold values from -6 to 6
- block_keep: int32 [16, 16], replicated, may hold values from 0 to 1, as said below
- scale_pick: int32 [3, 8], replicated, may hold values from 0 to 15
- scale_table: float32 [16, 64], replicated, may hold values from 1 to 16
- out_weight: bfloat16 [8192, 8192], P('tp', 'ctx'), may hold values from -0.09375 to 0.09375
Outputs:
- mixed: bfloat16 [3, 2048, 8192], P(None, 'ctx', 'tp')
The draws below stay inside these ranges and needn't reach their ends.
Inputs may be any that keep to these rules, and one draw needn't show every extreme that they name: block_keep is 0 above the diagonal and 1 on the diagonal and in the first column.
All inputs are finite; a program needn't handle non-finite values.
Results may differ from the reference program's by a relative error of at most 0.011.
Values may be sent and summed in bfloat16 or wider, within the bound.
A program may use at most 192 MiB of HBM per device.

```python
import math
import jax
import jax.numpy as jnp
from jax import lax

D = 8192
HEADS = 64
KV = 8
DH = 128
HALF = 64
CAND = 3
TABLE = 16
BLK = 128
TOKENS = 2048
NB = 16
N_TP = 4


def draw_keys(key, part):
    base = jnp.clip(jax.random.normal(jax.random.fold_in(key, 1), (TOKENS, KV * DH), jnp.float32), -8.0, 8.0)
    return base.astype(jnp.bfloat16)


def draw_queries(key, part):
    base = jnp.clip(jax.random.normal(jax.random.fold_in(key, 3), (TOKENS, HEADS * DH), jnp.float32), -8.0, 8.0)
    return base.astype(jnp.bfloat16)


def draw_block_keep(key, part):
    bits = jax.random.randint(jax.random.fold_in(key, 5), (NB, NB), 0, 2, dtype=jnp.int32)
    row = jnp.arange(NB)[:, None]
    col = jnp.arange(NB)[None, :]
    kept = jnp.where((col == row) | (col == 0), 1, bits)
    return jnp.where(col > row, 0, kept).astype(jnp.int32)


def place_ends(drawn, rng, smallest, largest):
    shape = drawn.shape
    index_at = [jax.random.randint(jax.random.fold_in(rng, axis), (), 0, shape[axis]) for axis in range(len(shape))]
    drawn = drawn.at[tuple(index_at)].set(smallest)
    longest = shape.index(max(shape))
    index_at[longest] = (index_at[longest] + 1) % shape[longest]
    return drawn.at[tuple(index_at)].set(largest)


def spiked(values, key, source, target, shards_of, factor):
    def block_of(position):
        return (jnp.arange(values.shape[position]) // (values.shape[position] // shards_of)).reshape((-1,) + (1,) * (values.ndim - 1 - position))

    near = jax.random.permutation(key, shards_of)[block_of(target)]
    second = (block_of(target) + shards_of // 2) % shards_of
    return jnp.where((block_of(source) == near) | (block_of(source) == second), factor * values, values)


def shard_levels(rng, dims, cuts, least, top_value):
    def one(dim, parts):
        steps = jax.random.uniform(jax.random.fold_in(jax.random.fold_in(rng, 6), dim), (parts,), jnp.float32, least / len(cuts), top_value / len(cuts))
        return jnp.repeat(jnp.exp(steps), dims[dim] // parts).reshape((-1,) + (1,) * (len(dims) - dim - 1))

    factor_of = one(*cuts[0])
    for cut in cuts[1:]:
        factor_of = factor_of * one(*cut)
    return factor_of


def noise(key, shape, width, bound, cuts=(), kind=jnp.bfloat16):
    drawn = jax.random.normal(key, shape, jnp.float32) * width
    if len(cuts) > 0:
        drawn = shard_levels(key, shape, cuts, -0.22, 0.18) * drawn
    return jnp.clip(drawn, min=-bound, max=bound).astype(kind)


def noise_with(rng, shape, scale, reach, cuts, heavy, kind=jnp.bfloat16):
    array = scale * jax.random.normal(rng, shape, jnp.float32)
    if cuts:
        array = array * shard_levels(rng, shape, cuts, -0.22, 0.18)
    return jnp.clip(spiked(array, jax.random.fold_in(rng, 3), *heavy), -reach, reach).astype(kind)


def setup_inputs(seed: int = 0) -> dict:
    seeds = jax.random.split(jax.random.key(seed), 8)
    return {
        "queries": draw_queries(jax.random.fold_in(seeds[7], 71), 0),
        "keys": draw_keys(jax.random.fold_in(seeds[7], 71), 0),
        "values": noise(seeds[2], (TOKENS, KV * DH), 1.0, 6.0, ((0, 8), (1, 4))),
        "block_keep": draw_block_keep(jax.random.fold_in(seeds[7], 71), 0),
        "scale_pick": place_ends(jax.random.randint(seeds[4], (CAND, KV), 0, TABLE), jax.random.fold_in(seeds[4], 1), 0, TABLE - 1).astype(jnp.int32),
        "scale_table": jnp.clip(jnp.exp(jax.random.uniform(seeds[5], (TABLE, HALF), jnp.float32, math.log(1.0), math.log(16.0))), 1.0, 16.0),
        "out_weight": noise_with(seeds[6], (HEADS * DH, D), (HEADS * DH) ** -0.5, 0.09375, ((0, 4), (1, 8)), (0, 1, 8, 2.0)),
    }


rope_theta = 500000.0


def inverse_freq():
    return 1.0 / (rope_theta ** (jnp.arange(DH // 2, dtype=jnp.float32) * 2.0 / DH))


def rotate(x, angle):
    cosine = jnp.cos(angle)
    sine = jnp.sin(angle)
    first = x[..., : DH // 2]
    second = x[..., DH // 2:]
    return jnp.concatenate([first * cosine - second * sine, second * cosine + first * sine], axis=-1)


def attend(qrot, krot, vals, block_keep):
    qblock = min(512, TOKENS)
    kpos = jnp.arange(TOKENS, dtype=jnp.int32)
    kf = krot.astype(jnp.float32)
    vf = vals.astype(jnp.float32)

    def one(index):
        start = (index * qblock).astype(jnp.int32)
        qpart = lax.dynamic_slice_in_dim(qrot, start, qblock, 0).astype(jnp.float32)
        score = jnp.einsum('qhd,kd->qhk', qpart, kf) * (DH ** -0.5)
        rows = lax.dynamic_slice_in_dim(block_keep, (start // BLK).astype(jnp.int32), qblock // BLK, 0)
        spread = jnp.repeat(jnp.repeat(rows, BLK, axis=0), BLK, axis=1)
        qpos = start + jnp.arange(qblock, dtype=jnp.int32)
        allowed = (kpos[None, :] <= qpos[:, None]) & (spread == 1)
        score = jnp.where(allowed[:, None, :], score, -1e30)
        top = jnp.max(score, axis=-1)
        weight = jnp.where(allowed[:, None, :], jnp.exp(score - top[..., None]), 0.0)
        total = jnp.sum(weight, axis=-1)
        rounded = lax.optimization_barrier(weight.astype(jnp.bfloat16)).astype(jnp.float32)
        output = jnp.einsum('qhk,kd->qhd', rounded, vf)
        return (output / total[..., None]).astype(jnp.bfloat16)

    blocks = lax.map(one, jnp.arange(TOKENS // qblock, dtype=jnp.int32))
    return blocks.reshape(TOKENS, -1)


def reference(queries, keys, values, block_keep, scale_pick, scale_table, out_weight):
    group = HEADS // KV
    posf = jnp.arange(TOKENS, dtype=jnp.float32)
    qheads = queries.reshape(TOKENS, KV, group, DH).astype(jnp.float32)
    kheads = keys.reshape(TOKENS, KV, DH).astype(jnp.float32)
    vheads = values.reshape(TOKENS, KV, DH)
    scales = scale_table[scale_pick]
    rows_tp = HEADS * DH // N_TP
    results = []
    for cand in range(CAND):
        freq = inverse_freq()[None, :] / scales[cand]
        angle = posf[:, None, None] * freq[None]
        qrot = rotate(qheads, angle[:, :, None, :]).astype(jnp.bfloat16)
        krot = rotate(kheads, angle).astype(jnp.bfloat16)
        pieces = [attend(qrot[:, g], krot[:, g], vheads[:, g], block_keep) for g in range(KV)]
        attn = jnp.concatenate(pieces, axis=1)
        total = jnp.zeros((TOKENS, D), jnp.float32)
        for owner in range(N_TP):
            part = jnp.dot(attn[:, owner * rows_tp:(owner + 1) * rows_tp], out_weight[owner * rows_tp:(owner + 1) * rows_tp], preferred_element_type=jnp.float32)
            total = total + lax.optimization_barrier(part.astype(jnp.bfloat16)).astype(jnp.float32)
        results.append(total.astype(jnp.bfloat16))
    return jnp.stack(results)
```

```python
import functools
import math

import jax
import jax.numpy as jnp
from jax import lax
from jax.experimental import pallas as pl
from jax.experimental.pallas import tpu as pltpu
from jax.sharding import PartitionSpec as P

DH = 128
BLK = 128
NC = 4
THETA = 500000.0
LOW = -1e30
MESH = pl.DeviceIdType.MESH
F32 = jnp.float32
BF16 = jnp.bfloat16


def chain_kernel(nctx, ntp, cands, kvh, group, tok,
           q_hbm, k_hbm, v_hbm, w_hbm, keep_ref, basec, bases, offc, offs,
           out_hbm,
           qv, kv, krot, vt, bias, attn, wbuf, pbuf, rbuf, obuf, ybuf,
           q_sem, kv_sem, kv_up, kv_y, kv_recv, w_local, w_send, w_recv,
           a_send, a_recv, p_send, p_recv, y_send, y_recv, o_sem):
    nk = nctx // 2
    me = lax.axis_index("ctx")
    t = lax.axis_index("tp")
    k = me // 2
    y = me % 2
    other = 1 - y
    cw = wbuf.shape[3]
    rows = cands * tok
    heads = kvh * group
    has_up = k + 1 < nk
    has_down = k > 0
    mate = (me + 1 - 2 * y, t)
    up = (jnp.minimum(k + 1, nk - 1) * 2 + y, t)
    down = (jnp.maximum(k - 1, 0) * 2 + y, t)

    def remote(src, dst, ssem, rsem, dev):
        return pltpu.make_async_remote_copy(
            src_ref=src, dst_ref=dst, send_sem=ssem, recv_sem=rsem,
            device_id=dev, device_id_type=MESH)

    q_copies = [
        pltpu.make_async_copy(q_hbm.at[:, pl.ds(h * DH, DH)], qv.at[h], q_sem.at[h])
        for h in range(heads)
    ]
    kv_copies = [
        pltpu.make_async_copy(src.at[:, pl.ds(g * DH, DH)], kv.at[me, i * kvh + g],
                              kv_sem.at[i * kvh + g])
        for i, src in enumerate((k_hbm, v_hbm)) for g in range(kvh)
    ]
    w_copies = [
        pltpu.make_async_copy(w_hbm.at[:, pl.ds(n * cw, cw)], wbuf.at[k, n], w_local.at[n])
        for n in range(NC)
    ]
    for c in kv_copies + q_copies:
        c.start()

    bar = pltpu.get_barrier_semaphore()
    pl.semaphore_signal(bar, inc=1, device_id=mate, device_id_type=MESH)
    for d in range(1, ntp):
        pl.semaphore_signal(bar, inc=1, device_id=(me, lax.rem(t + d, ntp)), device_id_type=MESH)

    @pl.when(has_up)
    def _():
        pl.semaphore_signal(bar, inc=1, device_id=up, device_id_type=MESH)

    @pl.when(has_down)
    def _():
        pl.semaphore_signal(bar, inc=1, device_id=down, device_id_type=MESH)

    pl.semaphore_wait(bar, ntp + has_up.astype(jnp.int32) + has_down.astype(jnp.int32))

    def kv_up_copy(j):
        s = 2 * j + y
        return remote(kv.at[s], kv.at[s], kv_up.at[j], kv_recv.at[s], up)

    def kv_mate_copy(j, col):
        s = 2 * j + col
        return remote(kv.at[s], kv.at[s], kv_y.at[j], kv_recv.at[s], mate)

    def kv_pass(j):
        @pl.when(has_up)
        def _():
            kv_up_copy(j).start()
        kv_mate_copy(j, y).start()

    def w_up_copy(j, n, src=None):
        return remote(wbuf.at[j, n] if src is None else src, wbuf.at[j, n],
                      w_send.at[0, j * NC + n], w_recv.at[j * NC + n], up)

    def w_down_copy(j, n, src=None):
        return remote(wbuf.at[j, n] if src is None else src, wbuf.at[j, n],
                      w_send.at[1, j * NC + n], w_recv.at[j * NC + n], down)

    for c in kv_copies:
        c.wait()
    kv_pass(k)
    @pl.when(has_down)
    def _():
        for n in range(NC):
            w_down_copy(k, n, w_hbm.at[:, pl.ds(n * cw, cw)]).start()
    for c in w_copies:
        c.start()

    kio = lax.broadcasted_iota(jnp.int32, (tok, tok), 0)
    qio = lax.broadcasted_iota(jnp.int32, (tok, tok), 1)
    nb = tok // BLK

    def make_bias(j, _):
        seen = jnp.zeros((tok, tok), jnp.int32)
        for a in range(nb):
            for b in range(nb):
                here = (qio // BLK == a) & (kio // BLK == b)
                seen = jnp.where(here, keep_ref[me * nb + a, j * nb + b], seen)
        ok = (seen == 1) & (kio + (j - me) * tok <= qio)
        bias[j] = jnp.where(ok, 0.0, LOW)
        return 0

    def tables(cg, j):
        bc, bs = basec[cg], bases[cg]
        oc = offc[cg, pl.ds(j, 1)]
        os = offs[cg, pl.ds(j, 1)]
        return bc * oc - bs * os, bs * oc + bc * os

    def turn(x, c, s):
        x = x.astype(F32)
        return (x * c + pltpu.roll(x, DH // 2, 1) * s).astype(BF16)

    for s in range(1, nk):
        @pl.when(k >= s)
        def _():
            kv_up_copy(k - s).wait_recv()
            kv_pass(k - s)

    @pl.when(has_up)
    def _():
        for n in range(NC):
            w_up_copy(k, n, w_hbm.at[:, pl.ds(n * cw, cw)]).start()

    def from_mate(j, _):
        kv_mate_copy(j, other).wait_recv()
        return 0

    lax.fori_loop(0, me + 1, make_bias, 0)
    lax.fori_loop(0, k + 1, from_mate, 0)

    def prepare(j, _):
        for g in range(kvh):
            vt[g, j] = jnp.transpose(kv[j, kvh + g].astype(F32)).astype(BF16)
            x = kv[j, g]
            for c in range(cands):
                cc, ss = tables(c * kvh + g, j)
                krot[c * kvh + g, j] = turn(x, cc, ss)
        return 0

    lax.fori_loop(0, me + 1, prepare, 0)
    for c in q_copies:
        c.wait()

    def forward(s, n):
        @pl.when((k >= s) & has_up)
        def _():
            w_up_copy(k - s, n).wait_recv()
            w_up_copy(k - s, n).start()

        @pl.when((k + s < nk) & has_down)
        def _():
            w_down_copy(k + s, n).wait_recv()
            w_down_copy(k + s, n).start()

    wide = 4
    per_c = kvh * group // wide
    c2 = DH ** (-0.5) * math.log2(math.e)

    def attn_copy(c, col):
        part = attn.at[col, pl.ds(c * tok, tok)]
        return remote(part, part, a_send.at[c], a_recv.at[c], mate)

    def candidate(c, _):
        def unit(i, _):
            g = i // (group // wide)
            cg = c * kvh + g
            h0 = wide * i
            cc, ss = tables(cg, me)
            qr = [turn(qv[h0 + d], cc, ss) for d in range(wide)]

            def step(j, state):
                kt = krot[cg, j]
                vv = vt[g, j]
                bj = bias[j]
                new = []
                sts = [lax.dot_general(kt, qr[d], (((1,), (1,)), ((), ())),
                                       preferred_element_type=F32) + bj
                       for d in range(wide)]
                for d in range(wide):
                    m, l, acc = state[d]
                    st = sts[d]
                    mn = jnp.maximum(m, jnp.max(st, axis=0, keepdims=True))
                    p = jnp.exp2((st - mn) * c2)
                    al = jnp.exp2((m - mn) * c2)
                    l = l * al + jnp.sum(p, axis=0, keepdims=True)
                    acc = acc * al + jnp.dot(vv, p.astype(BF16), preferred_element_type=F32)
                    new.append((mn, l, acc))
                return tuple(new)

            one = (jnp.full((1, tok), LOW, F32), jnp.zeros((1, tok), F32),
                   jnp.zeros((DH, tok), F32))
            state = lax.fori_loop(0, me + 1, step, (one,) * wide)
            for d in range(wide):
                m, l, acc = state[d]
                at = pl.multiple_of((h0 + d) * DH, DH)
                attn[y, pl.ds(pl.multiple_of(c * tok, tok), tok), pl.ds(at, DH)] = (
                    jnp.transpose(acc / l).astype(BF16))
            return 0

        lax.fori_loop(0, per_c, unit, 0)
        attn_copy(c, y).start()
        return 0

    lax.fori_loop(0, cands, candidate, 0)
    for c in w_copies:
        c.wait()
    for c in range(cands):
        attn_copy(c, other).wait_recv()

    def slot(j):
        return jnp.minimum(j - (j > t).astype(jnp.int32), nk - 2)

    def p_copy(j, n):
        return remote(pbuf.at[slot(j), n], rbuf.at[t, n], p_send.at[j, n], p_recv.at[t, n], (me, j))

    def p_arrive(src, n):
        return remote(rbuf.at[src, n], rbuf.at[src, n], p_send.at[src, n], p_recv.at[src, n],
                      (me, src))

    def y_copy(n, col):
        return remote(ybuf.at[n], obuf.at[col, n], y_send.at[n], y_recv.at[n], mate)

    def o_copy(col, n):
        return pltpu.make_async_copy(
            obuf.at[col, n],
            out_hbm.at[:, pl.ds(pl.multiple_of((col * NC + n) * cw, cw), cw)],
            o_sem.at[col, n])

    def project(j, n, dest):
        def block(half, _):
            dest[half] = jnp.dot(
                attn[half], wbuf[j, n], preferred_element_type=F32).astype(BF16)
            return 0
        lax.fori_loop(0, 2, block, 0)

    def compute(p, d, n):
        j = k - p if d == 0 else k + p
        ok = k >= p if d == 0 else k + p < nk
        fwd = has_up if d == 0 else has_down
        if p > 0:
            @pl.when(ok & jnp.logical_not(fwd))
            def _():
                (w_up_copy if d == 0 else w_down_copy)(j, n).wait_recv()
        @pl.when(ok & (j != t))
        def _():
            project(j, n, pbuf.at[slot(j), n])
            p_copy(j, n).start()

        @pl.when(ok & (j == t))
        def _():
            project(j, n, rbuf.at[t, n])

    def finish(n):
        for d in range(1, ntp):
            p_arrive(lax.rem(t + d, ntp), n).wait_recv()

        def total(half, r):
            acc = rbuf[0, n, half, pl.ds(r, BLK)].astype(F32)
            for src in range(1, ntp):
                acc = acc + rbuf[src, n, half, pl.ds(r, BLK)].astype(F32)
            return acc.astype(BF16)

        def block(b, _):
            r = pl.multiple_of(b * BLK, BLK)
            ybuf[n, pl.ds(r, BLK)] = total(other, r)
            return 0

        lax.fori_loop(0, rows // BLK, block, 0)
        y_copy(n, y).start()

        def block2(b, _):
            r = pl.multiple_of(b * BLK, BLK)
            obuf[y, n, pl.ds(r, BLK)] = total(y, r)
            return 0

        lax.fori_loop(0, rows // BLK, block2, 0)
        o_copy(y, n).start()

    for p in range(nk):
        mine = (t == k - p) | (t == k + p)

        if 0 < p < nk - 1:
            def pass_on(n, _):
                forward(p, n)
                return 0
            lax.fori_loop(0, NC, pass_on, 0)

        def chunk(n, _):
            compute(p, 0, n)
            if p > 0:
                compute(p, 1, n)

            @pl.when(mine & (n > 0))
            def _():
                finish(n - 1)
            return 0

        lax.fori_loop(0, NC, chunk, 0)

        @pl.when(mine)
        def _():
            finish(NC - 1)

    def drain(n, _):
        y_copy(n, other).wait_recv()
        o_copy(other, n).start()
        return 0

    lax.fori_loop(0, NC, drain, 0)

    def drain2(n, _):
        def sent(j, _):
            @pl.when(j != t)
            def _():
                p_copy(j, n).wait_send()
            return 0
        lax.fori_loop(0, nk, sent, 0)
        y_copy(n, y).wait_send()
        o_copy(y, n).wait()
        o_copy(other, n).wait()
        return 0

    lax.fori_loop(0, NC, drain2, 0)
    for c in range(cands):
        attn_copy(c, y).wait_send()

    def drain_kv(j, _):
        @pl.when(has_up)
        def _():
            kv_up_copy(j).wait_send()

            def each(n, _):
                w_up_copy(j, n).wait_send()
                return 0
            lax.fori_loop(0, NC, each, 0)
        kv_mate_copy(j, y).wait_send()
        return 0

    lax.fori_loop(0, k + 1, drain_kv, 0)

    @pl.when(has_down)
    def _():
        def drain_down(j, _):
            def each(n, _):
                w_down_copy(j, n).wait_send()
                return 0
            lax.fori_loop(0, NC, each, 0)
            return 0
        lax.fori_loop(k, nk, drain_down, 0)


def quad_fits(nctx, ntp, cands, cols):
    return nctx == 8 and ntp == 4 and cands == 3 and cols % (NC * DH) == 0


def quad_kernel(cands, kvh, group, tok,
                q_hbm, k_hbm, v_hbm, w_hbm, keep_ref, basec, bases, offc, offs,
                out_hbm,
                qv, kv, krot, vt, bias, attn, wbuf, give, kept, got, xgot,
                q_sem, kv_sem, kv_up, kv_y, kv_recv, w_local, w_send, w_recv,
                a_send, a_recv, g_send, g_recv, x_send, x_recv, o_send, o_recv):
    nz = 4
    me = lax.axis_index("ctx")
    t = lax.axis_index("tp")
    z, y = me // 2, me % 2
    zh, zl = z // 2, z % 2
    x, core = t // 2, t % 2
    cw = wbuf.shape[3]
    heads = kvh * group
    half = 2 * tok
    width = group * DH
    has_up = z + 1 < nz
    has_down = z > 0
    one = jnp.int32(1)

    mate = (z * 2 + 1 - y, t)
    up = (jnp.minimum(z + 1, nz - 1) * 2 + y, t)
    down = (jnp.maximum(z - 1, 0) * 2 + y, t)
    near = ((zh * 2 + 1 - zl) * 2 + y, t)
    far = (((1 - zh) * 2 + zl) * 2 + y, t)
    sibling = (me, x * 2 + 1 - core)
    across = (me, (1 - x) * 2 + core)
    at_home = (zl == core) & (core == y)

    def remote(src, dst, ssem, rsem, dev):
        return pltpu.make_async_remote_copy(
            src_ref=src, dst_ref=dst, send_sem=ssem, recv_sem=rsem,
            device_id=dev, device_id_type=MESH)

    q_copies = [
        pltpu.make_async_copy(q_hbm.at[:, pl.ds(h * DH, DH)], qv.at[h], q_sem.at[h])
        for h in range(heads)
    ]
    kv_copies = [
        pltpu.make_async_copy(src.at[:, pl.ds(g * DH, DH)], kv.at[me, i * kvh + g],
                              kv_sem.at[i * kvh + g])
        for i, src in enumerate((k_hbm, v_hbm)) for g in range(kvh)
    ]
    w_copies = [
        pltpu.make_async_copy(w_hbm.at[:, pl.ds(n * cw, cw)], wbuf.at[0, n], w_local.at[n])
        for n in range(NC)
    ]
    for c in kv_copies + q_copies:
        c.start()

    def out_target(zt):
        return ((zh * 2 + zt) * 2 + core, x * 2 + zl)

    def out_source(col):
        return ((zh * 2 + core) * 2 + col, x * 2 + y)

    bar = pltpu.get_barrier_semaphore()
    for dev in (mate, near, far, sibling, across):
        pl.semaphore_signal(bar, inc=1, device_id=dev, device_id_type=MESH)

    @pl.when(has_down)
    def _():
        pl.semaphore_signal(bar, inc=1, device_id=down, device_id_type=MESH)

    for col in range(2):
        @pl.when(jnp.logical_not(at_home & (col == y)))
        def _():
            pl.semaphore_signal(bar, inc=1, device_id=out_source(col), device_id_type=MESH)

    pl.semaphore_wait(bar, 7 + has_up.astype(jnp.int32) - at_home.astype(jnp.int32))

    def kv_up_copy(j):
        s = 2 * j + y
        return remote(kv.at[s], kv.at[s], kv_up.at[j], kv_recv.at[s], up)

    def kv_mate_copy(j, col):
        s = 2 * j + col
        return remote(kv.at[s], kv.at[s], kv_y.at[j], kv_recv.at[s], mate)

    def kv_pass(j):
        @pl.when(has_up)
        def _():
            kv_up_copy(j).start()
        kv_mate_copy(j, y).start()

    def w_copy(n):
        return remote(w_hbm.at[:, pl.ds(n * cw, cw)], wbuf.at[1, n],
                      w_send.at[n], w_recv.at[n], far)

    for c in kv_copies:
        c.wait()
    kv_pass(z)
    for n in range(NC):
        w_copy(n).start()
    for c in w_copies:
        c.start()

    kio = lax.broadcasted_iota(jnp.int32, (tok, tok), 0)
    qio = lax.broadcasted_iota(jnp.int32, (tok, tok), 1)
    nb = tok // BLK

    def make_bias(j, _):
        seen = jnp.zeros((tok, tok), jnp.int32)
        for a in range(nb):
            for b in range(nb):
                here = (qio // BLK == a) & (kio // BLK == b)
                seen = jnp.where(here, keep_ref[me * nb + a, j * nb + b], seen)
        ok = (seen == 1) & (kio + (j - me) * tok <= qio)
        bias[j] = jnp.where(ok, 0.0, LOW)
        return 0

    def tables(cg, j):
        bc, bs = basec[cg], bases[cg]
        oc = offc[cg, pl.ds(j, 1)]
        os = offs[cg, pl.ds(j, 1)]
        return bc * oc - bs * os, bs * oc + bc * os

    def turn(v, c, s):
        v = v.astype(F32)
        return (v * c + pltpu.roll(v, DH // 2, 1) * s).astype(BF16)

    for s in range(1, nz):
        @pl.when(z >= s)
        def _():
            kv_up_copy(z - s).wait_recv()
            kv_pass(z - s)

    def from_mate(j, _):
        kv_mate_copy(j, 1 - y).wait_recv()
        return 0

    lax.fori_loop(0, me + 1, make_bias, 0)
    lax.fori_loop(0, z + 1, from_mate, 0)

    def prepare(j, _):
        for g in range(kvh):
            vt[g, j] = jnp.transpose(kv[j, kvh + g].astype(F32)).astype(BF16)
            v = kv[j, g]
            for c in range(cands):
                cc, ss = tables(c * kvh + g, j)
                krot[c * kvh + g, j] = turn(v, cc, ss)
        return 0

    lax.fori_loop(0, me + 1, prepare, 0)
    for c in q_copies:
        c.wait()

    wide = 4
    per_piece = group // wide
    pieces = cands * kvh
    c2 = DH ** (-0.5) * math.log2(math.e)

    def part(i, ty, tz):
        c, g = i // kvh, i % kvh
        return attn.at[c, pl.ds(pl.multiple_of((ty * 2 + tz) * tok, tok), tok),
                       pl.ds(pl.multiple_of(g * width, width), width)]

    def a_copy(kind, i, ty, tz):
        p = part(i, ty, tz)
        return remote(p, p, a_send.at[kind, i], a_recv.at[kind, i], near if kind == 1 else mate)

    def relay(i):
        a_copy(1, i, y, 1 - zl).wait_recv()
        a_copy(2, i, y, 1 - zl).start()

    def piece(i, _):
        c, g = i // kvh, i % kvh
        cg = i

        def unit(v, _):
            h0 = g * group + wide * v
            cc, ss = tables(cg, me)
            qr = [turn(qv[h0 + d], cc, ss) for d in range(wide)]

            def step(j, state):
                kt = krot[cg, j]
                vv = vt[g, j]
                bj = bias[j]
                new = []
                sts = [lax.dot_general(kt, qr[d], (((1,), (1,)), ((), ())),
                                       preferred_element_type=F32) + bj
                       for d in range(wide)]
                for d in range(wide):
                    m, l, acc = state[d]
                    st = sts[d]
                    mn = jnp.maximum(m, jnp.max(st, axis=0, keepdims=True))
                    p = jnp.exp2((st - mn) * c2)
                    al = jnp.exp2((m - mn) * c2)
                    l = l * al + jnp.sum(p, axis=0, keepdims=True)
                    acc = acc * al + jnp.dot(vv, p.astype(BF16), preferred_element_type=F32)
                    new.append((mn, l, acc))
                return tuple(new)

            first = (jnp.full((1, tok), LOW, F32), jnp.zeros((1, tok), F32),
                     jnp.zeros((DH, tok), F32))
            state = lax.fori_loop(0, me + 1, step, (first,) * wide)
            for d in range(wide):
                m, l, acc = state[d]
                at = pl.multiple_of((h0 + d) * DH, DH)
                attn[c, pl.ds(pl.multiple_of((y * 2 + zl) * tok, tok), tok), pl.ds(at, DH)] = (
                    jnp.transpose(acc / l).astype(BF16))
            return 0

        lax.fori_loop(0, per_piece, unit, 0)
        a_copy(0, i, y, zl).start()
        a_copy(1, i, y, zl).start()

        @pl.when(i >= kvh)
        def _():
            relay(i - kvh)
        return 0

    lax.fori_loop(0, pieces, piece, 0)
    for c in w_copies:
        c.wait()

    def need_attn(c):
        for g in range(kvh):
            i = c * kvh + g
            a_copy(0, i, 1 - y, zl).wait_recv()
            a_copy(2, i, 1 - y, 1 - zl).wait_recv()

    first, late = NC * (cands - 1), (NC - 1) * (cands - 1)
    marks = (first, first + late, first + late + NC, first + late + NC + NC - 1)
    units = 2 * NC * cands

    def unit_of(u):
        m0, m1, m2, m3 = marks
        last = cands - 1
        w = jnp.where(u < m0, 0, jnp.where(u < m1, 1, jnp.where(u < m2, 0, 1)))
        n = jnp.where(u < m0, u % NC, jnp.where(u < m1, (u - m0) // last, jnp.where(
            u < m2, u - m1, jnp.where(u < m3, u - m2, NC - 1))))
        c = jnp.where(u < m0, u // NC, jnp.where(u < m1, (u - m0) % last, jnp.where(
            u < m3, last, u - m3)))
        return w, n, c

    def receives(w):
        return jnp.where(w == 0, zh, 1 - zh) == x

    def g_copy(u):
        return remote(give.at[u], got.at[u], g_send.at[u], g_recv.at[u], sibling)

    def x_copy(u, n, c):
        i = n * cands + c
        return remote(kept.at[u], xgot.at[i], x_send.at[i], x_recv.at[i], across)

    def o_ref(n, c, col):
        return out_hbm.at[pl.ds(pl.multiple_of(c * tok, tok), tok),
                          pl.ds(pl.multiple_of((col * NC + n) * cw, cw), cw)]

    def o_copy(u, n, c, zt):
        return remote(kept.at[u, pl.ds(zt * tok, tok)], o_ref(n, c, y),
                      o_send.at[zt, n * cands + c], o_recv.at[y, n * cands + c], out_target(zt))

    def o_local(u, n, c, zt):
        return pltpu.make_async_copy(kept.at[u, pl.ds(zt * tok, tok)], o_ref(n, c, y),
                                     o_send.at[zt, n * cands + c])

    def multiply(u):
        w, n, c = unit_of(u)

        def rows(i, _):
            r = pl.multiple_of(jnp.where(i == 0, 1 - core, core) * half, half)
            p = jnp.dot(attn[c, pl.ds(r, half)], wbuf[w, n],
                        preferred_element_type=F32).astype(BF16)

            @pl.when(i == 0)
            def _():
                give[u] = p
                g_copy(u).start()

            @pl.when(i == 1)
            def _():
                kept[u] = p
            return 0

        lax.fori_loop(0, 2, rows, 0)

    def pair(u):
        w, n, c = unit_of(u)

        @pl.when(jnp.logical_not(receives(w)))
        def _():
            g_copy(u).wait_recv()

            def block(b, _):
                r = pl.ds(pl.multiple_of(b * BLK, BLK), BLK)
                kept[u, r] = (kept[u, r].astype(F32) + got[u, r].astype(F32)).astype(BF16)
                return 0

            lax.fori_loop(0, half // BLK, block, 0)
            x_copy(u, n, c).start()

    def finish(u):
        w, n, c = unit_of(u)

        @pl.when(receives(w))
        def _():
            g_copy(u).wait_recv()
            i = n * cands + c
            x_copy(u, n, c).wait_recv()

            def block(b, _):
                r = pl.ds(pl.multiple_of(b * BLK, BLK), BLK)
                kept[u, r] = (kept[u, r].astype(F32) + got[u, r].astype(F32)
                              + xgot[i, r].astype(F32)).astype(BF16)
                return 0

            lax.fori_loop(0, half // BLK, block, 0)
            for zt in range(2):
                own = at_home & (zl == zt)

                @pl.when(own)
                def _():
                    o_local(u, n, c, zt).start()

                @pl.when(jnp.logical_not(own))
                def _():
                    o_copy(u, n, c, zt).start()

    def stretch(lo, hi, lag):
        def one_unit(u, _):
            @pl.when(u < hi)
            def _():
                multiply(u)

            @pl.when((u > lo) & (u <= hi))
            def _():
                pair(u - 1)

            @pl.when(u >= lo + lag)
            def _():
                finish(u - lag)
            return 0

        lax.fori_loop(lo, hi + lag, one_unit, 0)

    need_w = lambda n: w_copy(n).wait_recv()
    last = cands - 1
    need_attn(0)
    stretch(0, NC, 3)
    for c in range(1, last):
        need_attn(c)
        stretch(c * NC, (c + 1) * NC, 3)
    for n in range(NC - 1):
        need_w(n)
        if n == NC - 2:
            for g in range(kvh):
                relay(last * kvh + g)
        stretch(marks[0] + n * last, marks[0] + (n + 1) * last, 1)
    need_attn(last)
    stretch(marks[1], marks[3], 3)
    need_w(NC - 1)
    stretch(marks[3], units, 1)

    def arrived(i, _):
        n, c = i // cands, i % cands
        for col in range(2):
            @pl.when(jnp.logical_not(at_home & (col == y)))
            def _():
                remote(o_ref(n, c, col), o_ref(n, c, col), o_send.at[0, i], o_recv.at[col, i],
                       out_source(col)).wait_recv()
        return 0

    lax.fori_loop(0, NC * cands, arrived, 0)

    def drain(u, _):
        w, n, c = unit_of(u)
        g_copy(u).wait_send()

        @pl.when(receives(w))
        def _():
            for zt in range(2):
                own = at_home & (zl == zt)

                @pl.when(own)
                def _():
                    o_local(u, n, c, zt).wait()

                @pl.when(jnp.logical_not(own))
                def _():
                    o_copy(u, n, c, zt).wait_send()

        @pl.when(jnp.logical_not(receives(w)))
        def _():
            x_copy(u, n, c).wait_send()
        return 0

    lax.fori_loop(0, units, drain, 0)

    def drain_attn(i, _):
        a_copy(0, i, y, zl).wait_send()
        a_copy(1, i, y, zl).wait_send()
        a_copy(2, i, y, 1 - zl).wait_send()
        return 0

    lax.fori_loop(0, pieces, drain_attn, 0)
    for n in range(NC):
        w_copy(n).wait_send()

    def drain_kv(j, _):
        @pl.when(has_up)
        def _():
            kv_up_copy(j).wait_send()
        kv_mate_copy(j, y).wait_send()
        return 0

    lax.fori_loop(0, z + 1, drain_kv, 0)


def quad(nctx, ntp, cands, kvh, group, tok, rw, cols,
         queries, keys, values, out_weight, block_keep, basec, bases, offc, offs):
    heads = kvh * group
    cg = cands * kvh
    cw = cols // NC
    units = 2 * NC * cands
    hbm = pl.BlockSpec(memory_space=pl.ANY)
    vmem = pl.BlockSpec(memory_space=pltpu.VMEM)
    dma = pltpu.SemaphoreType.DMA
    return pl.pallas_call(
        functools.partial(quad_kernel, cands, kvh, group, tok),
        out_shape=jax.ShapeDtypeStruct((cands * tok, 2 * cols), BF16),
        in_specs=[hbm] * 4 + [pl.BlockSpec(memory_space=pltpu.SMEM)] + [vmem] * 4,
        out_specs=hbm,
        scratch_shapes=[
            pltpu.VMEM((heads, tok, DH), BF16),
            pltpu.VMEM((nctx, 2 * kvh, tok, DH), BF16),
            pltpu.VMEM((cg, nctx, tok, DH), BF16),
            pltpu.VMEM((kvh, nctx, DH, tok), BF16),
            pltpu.VMEM((nctx, tok, tok), F32),
            pltpu.VMEM((cands, 4 * tok, rw), BF16),
            pltpu.VMEM((2, NC, rw, cw), BF16),
            pltpu.VMEM((units, 2 * tok, cw), BF16),
            pltpu.VMEM((units, 2 * tok, cw), BF16),
            pltpu.VMEM((units, 2 * tok, cw), BF16),
            pltpu.VMEM((NC * cands, 2 * tok, cw), BF16),
            dma((heads,)), dma((2 * kvh,)), dma((nctx // 2,)), dma((nctx // 2,)), dma((nctx,)),
            dma((NC,)), dma((NC,)), dma((NC,)),
            dma((3, cg)), dma((3, cg)), dma((units,)), dma((units,)),
            dma((NC * cands,)), dma((NC * cands,)), dma((2, NC * cands)), dma((2, NC * cands)),
        ],
        compiler_params=pltpu.CompilerParams(
            collective_id=0, has_side_effects=True, vmem_limit_bytes=63 * 2**20),
        cost_estimate=pl.CostEstimate(
            flops=4 * nctx * tok * tok * heads * cands * DH + 4 * 4 * cands * tok * rw * cols,
            bytes_accessed=4 * rw * cols * 2,
            transcendentals=nctx * tok * tok * heads * cands),
        name="attend_project",
    )(queries, keys, values, out_weight, block_keep, basec, bases, offc, offs)


def body(nctx, ntp, queries, keys, values, block_keep, scale_pick, scale_table, out_weight):
    tok = queries.shape[0]
    kvh = keys.shape[1] // DH
    group = queries.shape[1] // (kvh * DH)
    cands = scale_pick.shape[0]
    kv_all = scale_pick.shape[1]
    table_rows = scale_table.shape[0]
    rw, cols = out_weight.shape
    nk = nctx // 2
    cw = cols // NC
    heads = kvh * group
    rows = cands * tok
    here = lax.axis_index("tp") * kvh + jnp.arange(kvh, dtype=jnp.int32)
    select = jnp.arange(kv_all, dtype=jnp.int32)[None, :] == here[:, None]
    picks = jnp.sum(jnp.where(select[None], scale_pick[:, None, :], 0), axis=-1)
    hit = picks[..., None] == jnp.arange(table_rows, dtype=jnp.int32)
    scales = jnp.sum(jnp.where(hit[..., None], scale_table[None, None], 0.0), axis=2)
    inv = 1.0 / THETA ** (jnp.arange(DH // 2, dtype=F32) * 2.0 / DH)
    freq = (inv / scales).reshape(cands * kvh, 1, DH // 2)

    def table(positions):
        angle = positions.astype(F32)[None, :, None] * freq
        c, s = jnp.cos(angle), jnp.sin(angle)
        return jnp.concatenate([c, c], -1), jnp.concatenate([-s, s], -1)

    basec, bases = table(jnp.arange(tok, dtype=jnp.int32))
    offc, offs = table(jnp.arange(nctx, dtype=jnp.int32) * tok)
    cg = cands * kvh
    hbm = pl.BlockSpec(memory_space=pl.ANY)
    vmem = pl.BlockSpec(memory_space=pltpu.VMEM)
    dma = pltpu.SemaphoreType.DMA
    if quad_fits(nctx, ntp, cands, cols):
        out = quad(nctx, ntp, cands, kvh, group, tok, rw, cols,
                   queries, keys, values, out_weight, block_keep, basec, bases, offc, offs)
        return out.reshape(cands, tok, 2 * cols)
    flops = 4 * nctx * tok * tok * heads * cands * DH + 4 * rows * rw * cols * nk
    out = pl.pallas_call(
        functools.partial(chain_kernel, nctx, ntp, cands, kvh, group, tok),
        out_shape=jax.ShapeDtypeStruct((rows, 2 * cols), BF16),
        in_specs=[hbm] * 4 + [pl.BlockSpec(memory_space=pltpu.SMEM)] + [vmem] * 4,
        out_specs=hbm,
        scratch_shapes=[
            pltpu.VMEM((heads, tok, DH), BF16),
            pltpu.VMEM((nctx, 2 * kvh, tok, DH), BF16),
            pltpu.VMEM((cg, nctx, tok, DH), BF16),
            pltpu.VMEM((kvh, nctx, DH, tok), BF16),
            pltpu.VMEM((nctx, tok, tok), F32),
            pltpu.VMEM((2, rows, rw), BF16),
            pltpu.VMEM((nk, NC, rw, cw), BF16),
            pltpu.VMEM((nk - 1, NC, 2, rows, cw), BF16),
            pltpu.VMEM((ntp, NC, 2, rows, cw), BF16),
            pltpu.VMEM((2, NC, rows, cw), BF16),
            pltpu.VMEM((NC, rows, cw), BF16),
            dma((heads,)), dma((2 * kvh,)), dma((nk,)), dma((nk,)), dma((nctx,)),
            dma((NC,)), dma((2, nk * NC)), dma((nk * NC,)),
            dma((cands,)), dma((cands,)), dma((nk, NC)), dma((ntp, NC)),
            dma((NC,)), dma((NC,)), dma((2, NC)),
        ],
        compiler_params=pltpu.CompilerParams(
            collective_id=0, has_side_effects=True, vmem_limit_bytes=63 * 2**20),
        cost_estimate=pl.CostEstimate(
            flops=flops, bytes_accessed=4 * rw * cols * nk,
            transcendentals=nctx * tok * tok * heads * cands),
        name="attend_project",
    )(queries, keys, values, out_weight, block_keep, basec, bases, offc, offs)
    return out.reshape(cands, tok, 2 * cols)


def solution(mesh):
    return jax.shard_map(
        functools.partial(body, mesh.shape["ctx"], mesh.shape["tp"]),
        mesh=mesh,
        in_specs=(P("ctx", "tp"), P("ctx", "tp"), P("ctx", "tp"), P(), P(), P(), P("tp", "ctx")),
        out_specs=P(None, "ctx", "tp"),
        check_vma=False,
    )
```

```python
import functools
import math

import jax
import jax.numpy as jnp
from jax import lax
from jax.experimental import pallas as pl
from jax.experimental.pallas import tpu as pltpu
from jax.sharding import PartitionSpec as P

DH = 128
BLK = 128
NC = 4
THETA = 500000.0
LOW = -1e30
MESH = pl.DeviceIdType.MESH
F32 = jnp.float32
BF16 = jnp.bfloat16


def chain_kernel(nctx, ntp, cands, kvh, group, tok,
           q_hbm, k_hbm, v_hbm, w_hbm, keep_ref, basec, bases, offc, offs,
           out_hbm,
           qv, kv, krot, vt, bias, attn, wbuf, pbuf, rbuf, obuf, ybuf,
           q_sem, kv_sem, kv_up, kv_y, kv_recv, w_local, w_send, w_recv,
           a_send, a_recv, p_send, p_recv, y_send, y_recv, o_sem):
    nk = nctx // 2
    me = lax.axis_index("ctx")
    t = lax.axis_index("tp")
    k = me // 2
    y = me % 2
    other = 1 - y
    cw = wbuf.shape[3]
    rows = cands * tok
    heads = kvh * group
    has_up = k + 1 < nk
    has_down = k > 0
    mate = (me + 1 - 2 * y, t)
    up = (jnp.minimum(k + 1, nk - 1) * 2 + y, t)
    down = (jnp.maximum(k - 1, 0) * 2 + y, t)

    def remote(src, dst, ssem, rsem, dev):
        return pltpu.make_async_remote_copy(
            src_ref=src, dst_ref=dst, send_sem=ssem, recv_sem=rsem,
            device_id=dev, device_id_type=MESH)

    q_copies = [
        pltpu.make_async_copy(q_hbm.at[:, pl.ds(h * DH, DH)], qv.at[h], q_sem.at[h])
        for h in range(heads)
    ]
    kv_copies = [
        pltpu.make_async_copy(src.at[:, pl.ds(g * DH, DH)], kv.at[me, i * kvh + g],
                              kv_sem.at[i * kvh + g])
        for i, src in enumerate((k_hbm, v_hbm)) for g in range(kvh)
    ]
    w_copies = [
        pltpu.make_async_copy(w_hbm.at[:, pl.ds(n * cw, cw)], wbuf.at[k, n], w_local.at[n])
        for n in range(NC)
    ]
    for c in kv_copies + q_copies:
        c.start()

    bar = pltpu.get_barrier_semaphore()
    pl.semaphore_signal(bar, inc=1, device_id=mate, device_id_type=MESH)
    for d in range(1, ntp):
        pl.semaphore_signal(bar, inc=1, device_id=(me, lax.rem(t + d, ntp)), device_id_type=MESH)

    @pl.when(has_up)
    def _():
        pl.semaphore_signal(bar, inc=1, device_id=up, device_id_type=MESH)

    @pl.when(has_down)
    def _():
        pl.semaphore_signal(bar, inc=1, device_id=down, device_id_type=MESH)

    pl.semaphore_wait(bar, ntp + has_up.astype(jnp.int32) + has_down.astype(jnp.int32))

    def kv_up_copy(j):
        s = 2 * j + y
        return remote(kv.at[s], kv.at[s], kv_up.at[j], kv_recv.at[s], up)

    def kv_mate_copy(j, col):
        s = 2 * j + col
        return remote(kv.at[s], kv.at[s], kv_y.at[j], kv_recv.at[s], mate)

    def kv_pass(j):
        @pl.when(has_up)
        def _():
            kv_up_copy(j).start()
        kv_mate_copy(j, y).start()

    def w_up_copy(j, n, src=None):
        return remote(wbuf.at[j, n] if src is None else src, wbuf.at[j, n],
                      w_send.at[0, j * NC + n], w_recv.at[j * NC + n], up)

    def w_down_copy(j, n, src=None):
        return remote(wbuf.at[j, n] if src is None else src, wbuf.at[j, n],
                      w_send.at[1, j * NC + n], w_recv.at[j * NC + n], down)

    for c in kv_copies:
        c.wait()
    kv_pass(k)
    @pl.when(has_down)
    def _():
        for n in range(NC):
            w_down_copy(k, n, w_hbm.at[:, pl.ds(n * cw, cw)]).start()
    for c in w_copies:
        c.start()

    kio = lax.broadcasted_iota(jnp.int32, (tok, tok), 0)
    qio = lax.broadcasted_iota(jnp.int32, (tok, tok), 1)
    nb = tok // BLK

    def make_bias(j, _):
        seen = jnp.zeros((tok, tok), jnp.int32)
        for a in range(nb):
            for b in range(nb):
                here = (qio // BLK == a) & (kio // BLK == b)
                seen = jnp.where(here, keep_ref[me * nb + a, j * nb + b], seen)
        ok = (seen == 1) & (kio + (j - me) * tok <= qio)
        bias[j] = jnp.where(ok, 0.0, LOW)
        return 0

    def tables(cg, j):
        bc, bs = basec[cg], bases[cg]
        oc = offc[cg, pl.ds(j, 1)]
        os = offs[cg, pl.ds(j, 1)]
        return bc * oc - bs * os, bs * oc + bc * os

    def turn(x, c, s):
        x = x.astype(F32)
        return (x * c + pltpu.roll(x, DH // 2, 1) * s).astype(BF16)

    for s in range(1, nk):
        @pl.when(k >= s)
        def _():
            kv_up_copy(k - s).wait_recv()
            kv_pass(k - s)

    @pl.when(has_up)
    def _():
        for n in range(NC):
            w_up_copy(k, n, w_hbm.at[:, pl.ds(n * cw, cw)]).start()

    def from_mate(j, _):
        kv_mate_copy(j, other).wait_recv()
        return 0

    lax.fori_loop(0, me + 1, make_bias, 0)
    lax.fori_loop(0, k + 1, from_mate, 0)

    def prepare(j, _):
        for g in range(kvh):
            vt[g, j] = jnp.transpose(kv[j, kvh + g].astype(F32)).astype(BF16)
            x = kv[j, g]
            for c in range(cands):
                cc, ss = tables(c * kvh + g, j)
                krot[c * kvh + g, j] = turn(x, cc, ss)
        return 0

    lax.fori_loop(0, me + 1, prepare, 0)
    for c in q_copies:
        c.wait()

    def forward(s, n):
        @pl.when((k >= s) & has_up)
        def _():
            w_up_copy(k - s, n).wait_recv()
            w_up_copy(k - s, n).start()

        @pl.when((k + s < nk) & has_down)
        def _():
            w_down_copy(k + s, n).wait_recv()
            w_down_copy(k + s, n).start()

    wide = 4
    per_c = kvh * group // wide
    c2 = DH ** (-0.5) * math.log2(math.e)

    def attn_copy(c, col):
        part = attn.at[col, pl.ds(c * tok, tok)]
        return remote(part, part, a_send.at[c], a_recv.at[c], mate)

    def candidate(c, _):
        def unit(i, _):
            g = i // (group // wide)
            cg = c * kvh + g
            h0 = wide * i
            cc, ss = tables(cg, me)
            qr = [turn(qv[h0 + d], cc, ss) for d in range(wide)]

            def step(j, state):
                kt = krot[cg, j]
                vv = vt[g, j]
                bj = bias[j]
                new = []
                sts = [lax.dot_general(kt, qr[d], (((1,), (1,)), ((), ())),
                                       preferred_element_type=F32) + bj
                       for d in range(wide)]
                for d in range(wide):
                    m, l, acc = state[d]
                    st = sts[d]
                    mn = jnp.maximum(m, jnp.max(st, axis=0, keepdims=True))
                    p = jnp.exp2((st - mn) * c2)
                    al = jnp.exp2((m - mn) * c2)
                    l = l * al + jnp.sum(p, axis=0, keepdims=True)
                    acc = acc * al + jnp.dot(vv, p.astype(BF16), preferred_element_type=F32)
                    new.append((mn, l, acc))
                return tuple(new)

            one = (jnp.full((1, tok), LOW, F32), jnp.zeros((1, tok), F32),
                   jnp.zeros((DH, tok), F32))
            state = lax.fori_loop(0, me + 1, step, (one,) * wide)
            for d in range(wide):
                m, l, acc = state[d]
                at = pl.multiple_of((h0 + d) * DH, DH)
                attn[y, pl.ds(pl.multiple_of(c * tok, tok), tok), pl.ds(at, DH)] = (
                    jnp.transpose(acc / l).astype(BF16))
            return 0

        lax.fori_loop(0, per_c, unit, 0)
        attn_copy(c, y).start()
        return 0

    lax.fori_loop(0, cands, candidate, 0)
    for c in w_copies:
        c.wait()
    for c in range(cands):
        attn_copy(c, other).wait_recv()

    def slot(j):
        return jnp.minimum(j - (j > t).astype(jnp.int32), nk - 2)

    def p_copy(j, n):
        return remote(pbuf.at[slot(j), n], rbuf.at[t, n], p_send.at[j, n], p_recv.at[t, n], (me, j))

    def p_arrive(src, n):
        return remote(rbuf.at[src, n], rbuf.at[src, n], p_send.at[src, n], p_recv.at[src, n],
                      (me, src))

    def y_copy(n, col):
        return remote(ybuf.at[n], obuf.at[col, n], y_send.at[n], y_recv.at[n], mate)

    def o_copy(col, n):
        return pltpu.make_async_copy(
            obuf.at[col, n],
            out_hbm.at[:, pl.ds(pl.multiple_of((col * NC + n) * cw, cw), cw)],
            o_sem.at[col, n])

    def project(j, n, dest):
        def block(half, _):
            dest[half] = jnp.dot(
                attn[half], wbuf[j, n], preferred_element_type=F32).astype(BF16)
            return 0
        lax.fori_loop(0, 2, block, 0)

    def compute(p, d, n):
        j = k - p if d == 0 else k + p
        ok = k >= p if d == 0 else k + p < nk
        fwd = has_up if d == 0 else has_down
        if p > 0:
            @pl.when(ok & jnp.logical_not(fwd))
            def _():
                (w_up_copy if d == 0 else w_down_copy)(j, n).wait_recv()
        @pl.when(ok & (j != t))
        def _():
            project(j, n, pbuf.at[slot(j), n])
            p_copy(j, n).start()

        @pl.when(ok & (j == t))
        def _():
            project(j, n, rbuf.at[t, n])

    def finish(n):
        for d in range(1, ntp):
            p_arrive(lax.rem(t + d, ntp), n).wait_recv()

        def total(half, r):
            acc = rbuf[0, n, half, pl.ds(r, BLK)].astype(F32)
            for src in range(1, ntp):
                acc = acc + rbuf[src, n, half, pl.ds(r, BLK)].astype(F32)
            return acc.astype(BF16)

        def block(b, _):
            r = pl.multiple_of(b * BLK, BLK)
            ybuf[n, pl.ds(r, BLK)] = total(other, r)
            return 0

        lax.fori_loop(0, rows // BLK, block, 0)
        y_copy(n, y).start()

        def block2(b, _):
            r = pl.multiple_of(b * BLK, BLK)
            obuf[y, n, pl.ds(r, BLK)] = total(y, r)
            return 0

        lax.fori_loop(0, rows // BLK, block2, 0)
        o_copy(y, n).start()

    for p in range(nk):
        mine = (t == k - p) | (t == k + p)

        if 0 < p < nk - 1:
            def pass_on(n, _):
                forward(p, n)
                return 0
            lax.fori_loop(0, NC, pass_on, 0)

        def chunk(n, _):
            compute(p, 0, n)
            if p > 0:
                compute(p, 1, n)

            @pl.when(mine & (n > 0))
            def _():
                finish(n - 1)
            return 0

        lax.fori_loop(0, NC, chunk, 0)

        @pl.when(mine)
        def _():
            finish(NC - 1)

    def drain(n, _):
        y_copy(n, other).wait_recv()
        o_copy(other, n).start()
        return 0

    lax.fori_loop(0, NC, drain, 0)

    def drain2(n, _):
        def sent(j, _):
            @pl.when(j != t)
            def _():
                p_copy(j, n).wait_send()
            return 0
        lax.fori_loop(0, nk, sent, 0)
        y_copy(n, y).wait_send()
        o_copy(y, n).wait()
        o_copy(other, n).wait()
        return 0

    lax.fori_loop(0, NC, drain2, 0)
    for c in range(cands):
        attn_copy(c, y).wait_send()

    def drain_kv(j, _):
        @pl.when(has_up)
        def _():
            kv_up_copy(j).wait_send()

            def each(n, _):
                w_up_copy(j, n).wait_send()
                return 0
            lax.fori_loop(0, NC, each, 0)
        kv_mate_copy(j, y).wait_send()
        return 0

    lax.fori_loop(0, k + 1, drain_kv, 0)

    @pl.when(has_down)
    def _():
        def drain_down(j, _):
            def each(n, _):
                w_down_copy(j, n).wait_send()
                return 0
            lax.fori_loop(0, NC, each, 0)
            return 0
        lax.fori_loop(k, nk, drain_down, 0)


ISSUE = (
    (0, 3, 5, 7),
    (1, 1, 1, 1),
    (1, 1, 1, 1),
    (0, 3, 5, 7),
)
LAG = 5
ORDER = (
    ((0, 0, 0), (1, 0, 0), (0, 1, 0), (0, 2, 0), (0, 3, 0)),
    ((0, 0, 1), (1, 0, 1), (0, 1, 1), (1, 1, 0), (0, 2, 1), (1, 1, 1), (0, 3, 1)),
    ((1, 2, 0), (1, 2, 1)),
    ((0, 0, 2), (1, 0, 2), (0, 1, 2), (1, 1, 2), (0, 2, 2), (1, 2, 2), (0, 3, 2)),
    ((1, 3, 0), (1, 3, 1), (1, 3, 2)),
)


def quad_fits(nctx, ntp, cands, cols):
    return nctx == 8 and ntp == 4 and cands == 3 and cols % (NC * DH) == 0


def quad_kernel(cands, kvh, group, tok,
                q_hbm, k_hbm, v_hbm, w_hbm, keep_ref, basec, bases, offc, offs,
                out_hbm,
                qv, kv, krot, vt, bias, attn, wbuf, give, kept, got, xgot,
                q_sem, kv_sem, kv_up, kv_y, kv_recv, w_local, w_send, w_recv,
                a_send, a_recv, g_send, g_recv, x_send, x_recv, o_send, o_recv):
    nz = 4
    me = lax.axis_index("ctx")
    t = lax.axis_index("tp")
    z, y = me // 2, me % 2
    zh, zl = z // 2, z % 2
    x, core = t // 2, t % 2
    cw = wbuf.shape[3]
    heads = kvh * group
    half = 2 * tok
    width = group * DH
    has_up = z + 1 < nz
    has_down = z > 0
    one = jnp.int32(1)

    mate = (z * 2 + 1 - y, t)
    up = (jnp.minimum(z + 1, nz - 1) * 2 + y, t)
    down = (jnp.maximum(z - 1, 0) * 2 + y, t)
    near = ((zh * 2 + 1 - zl) * 2 + y, t)
    far = (((1 - zh) * 2 + zl) * 2 + y, t)
    sibling = (me, x * 2 + 1 - core)
    across = (me, (1 - x) * 2 + core)
    at_home = (zl == core) & (core == y)

    def remote(src, dst, ssem, rsem, dev):
        return pltpu.make_async_remote_copy(
            src_ref=src, dst_ref=dst, send_sem=ssem, recv_sem=rsem,
            device_id=dev, device_id_type=MESH)

    q_copies = [
        pltpu.make_async_copy(q_hbm.at[:, pl.ds(h * DH, DH)], qv.at[h], q_sem.at[h])
        for h in range(heads)
    ]
    kv_copies = [
        pltpu.make_async_copy(src.at[:, pl.ds(g * DH, DH)], kv.at[me, i * kvh + g],
                              kv_sem.at[i * kvh + g])
        for i, src in enumerate((k_hbm, v_hbm)) for g in range(kvh)
    ]
    w_copies = [
        pltpu.make_async_copy(w_hbm.at[:, pl.ds(n * cw, cw)], wbuf.at[0, n], w_local.at[n])
        for n in range(NC)
    ]
    for c in kv_copies + q_copies:
        c.start()

    def out_target(zt):
        return ((zh * 2 + zt) * 2 + core, x * 2 + zl)

    def out_source(col):
        return ((zh * 2 + core) * 2 + col, x * 2 + y)

    bar = pltpu.get_barrier_semaphore()
    for dev in (mate, near, far, sibling, across):
        pl.semaphore_signal(bar, inc=1, device_id=dev, device_id_type=MESH)

    @pl.when(has_down)
    def _():
        pl.semaphore_signal(bar, inc=1, device_id=down, device_id_type=MESH)

    for col in range(2):
        @pl.when(jnp.logical_not(at_home & (col == y)))
        def _():
            pl.semaphore_signal(bar, inc=1, device_id=out_source(col), device_id_type=MESH)

    pl.semaphore_wait(bar, 7 + has_up.astype(jnp.int32) - at_home.astype(jnp.int32))

    def kv_up_copy(j):
        s = 2 * j + y
        return remote(kv.at[s], kv.at[s], kv_up.at[j], kv_recv.at[s], up)

    def kv_mate_copy(j, col):
        s = 2 * j + col
        return remote(kv.at[s], kv.at[s], kv_y.at[j], kv_recv.at[s], mate)

    def kv_pass(j):
        @pl.when(has_up)
        def _():
            kv_up_copy(j).start()
        kv_mate_copy(j, y).start()

    def w_copy(n):
        return remote(w_hbm.at[:, pl.ds(n * cw, cw)], wbuf.at[1, n],
                      w_send.at[n], w_recv.at[n], far)

    def issue(point):
        for zz in range(nz):
            for n in range(NC):
                if ISSUE[zz][n] in (point if isinstance(point, range) else (point,)):
                    here = z == zz

                    @pl.when(here)
                    def _():
                        w_copy(n).start()

    for c in kv_copies:
        c.wait()
    kv_pass(z)
    issue(0)
    for c in w_copies:
        c.start()

    kio = lax.broadcasted_iota(jnp.int32, (tok, tok), 0)
    qio = lax.broadcasted_iota(jnp.int32, (tok, tok), 1)
    nb = tok // BLK

    def make_bias(j, _):
        seen = jnp.zeros((tok, tok), jnp.int32)
        for a in range(nb):
            for b in range(nb):
                here = (qio // BLK == a) & (kio // BLK == b)
                seen = jnp.where(here, keep_ref[me * nb + a, j * nb + b], seen)
        ok = (seen == 1) & (kio + (j - me) * tok <= qio)
        bias[j] = jnp.where(ok, 0.0, LOW)
        return 0

    def tables(cg, j):
        bc, bs = basec[cg], bases[cg]
        oc = offc[cg, pl.ds(j, 1)]
        os = offs[cg, pl.ds(j, 1)]
        return bc * oc - bs * os, bs * oc + bc * os

    def turn(v, c, s):
        v = v.astype(F32)
        return (v * c + pltpu.roll(v, DH // 2, 1) * s).astype(BF16)

    for s in range(1, nz):
        @pl.when(z >= s)
        def _():
            kv_up_copy(z - s).wait_recv()
            kv_pass(z - s)

    issue(1)

    def from_mate(j, _):
        kv_mate_copy(j, 1 - y).wait_recv()
        return 0

    lax.fori_loop(0, me + 1, make_bias, 0)
    lax.fori_loop(0, z + 1, from_mate, 0)

    def prepare(j, _):
        for g in range(kvh):
            vt[g, j] = jnp.transpose(kv[j, kvh + g].astype(F32)).astype(BF16)
            v = kv[j, g]
            for c in range(cands):
                cc, ss = tables(c * kvh + g, j)
                krot[c * kvh + g, j] = turn(v, cc, ss)
        return 0

    lax.fori_loop(0, me + 1, prepare, 0)
    for c in q_copies:
        c.wait()

    wide = 4
    per_piece = group // wide
    pieces = cands * kvh
    c2 = DH ** (-0.5) * math.log2(math.e)

    def part(i, ty, tz):
        c, g = i // kvh, i % kvh
        return attn.at[c, pl.ds(pl.multiple_of((ty * 2 + tz) * tok, tok), tok),
                       pl.ds(pl.multiple_of(g * width, width), width)]

    def a_copy(kind, i, ty, tz):
        p = part(i, ty, tz)
        return remote(p, p, a_send.at[kind, i], a_recv.at[kind, i], near if kind == 1 else mate)

    def relay(i):
        a_copy(1, i, y, 1 - zl).wait_recv()
        a_copy(2, i, y, 1 - zl).start()

    def piece(i, _):
        c, g = i // kvh, i % kvh
        cg = i

        def unit(v, _):
            h0 = g * group + wide * v
            cc, ss = tables(cg, me)
            qr = [turn(qv[h0 + d], cc, ss) for d in range(wide)]

            def step(j, state):
                kt = krot[cg, j]
                vv = vt[g, j]
                bj = bias[j]
                new = []
                sts = [lax.dot_general(kt, qr[d], (((1,), (1,)), ((), ())),
                                       preferred_element_type=F32) + bj
                       for d in range(wide)]
                for d in range(wide):
                    m, l, acc = state[d]
                    st = sts[d]
                    mn = jnp.maximum(m, jnp.max(st, axis=0, keepdims=True))
                    p = jnp.exp2((st - mn) * c2)
                    al = jnp.exp2((m - mn) * c2)
                    l = l * al + jnp.sum(p, axis=0, keepdims=True)
                    acc = acc * al + jnp.dot(vv, p.astype(BF16), preferred_element_type=F32)
                    new.append((mn, l, acc))
                return tuple(new)

            first = (jnp.full((1, tok), LOW, F32), jnp.zeros((1, tok), F32),
                     jnp.zeros((DH, tok), F32))
            state = lax.fori_loop(0, me + 1, step, (first,) * wide)
            for d in range(wide):
                m, l, acc = state[d]
                at = pl.multiple_of((h0 + d) * DH, DH)
                attn[c, pl.ds(pl.multiple_of((y * 2 + zl) * tok, tok), tok), pl.ds(at, DH)] = (
                    jnp.transpose(acc / l).astype(BF16))
            return 0

        lax.fori_loop(0, per_piece, unit, 0)
        a_copy(0, i, y, zl).start()
        a_copy(1, i, y, zl).start()

        for zz in range(nz):
            for n in range(NC):
                if 2 <= ISSUE[zz][n] < 2 + pieces:
                    @pl.when((z == zz) & (i == ISSUE[zz][n] - 2))
                    def _():
                        w_copy(n).start()

        @pl.when((zl == 0) & (i >= kvh))
        def _():
            relay(i - kvh)

        @pl.when(zl == 1)
        def _():
            relay(i)
        return 0

    lax.fori_loop(0, pieces, piece, 0)
    issue(2 + pieces)

    def relay_rest(c):
        @pl.when(zl == 0)
        def _():
            for g in range(kvh):
                relay(c * kvh + g)
    for c in w_copies:
        c.wait()

    def need_attn(c):
        for g in range(kvh):
            i = c * kvh + g
            a_copy(0, i, 1 - y, zl).wait_recv()
            a_copy(2, i, 1 - y, 1 - zl).wait_recv()

    units = 2 * NC * cands
    table = [v for seg in ORDER for v in seg]

    def unit_of(u):
        low = u < 12
        sh = 2 * jnp.where(low, u, u - 12)

        def pick(k):
            words = [sum(v[k] << (2 * i) for i, v in enumerate(table[a:a + 12])) for a in (0, 12)]
            return lax.shift_right_logical(
                jnp.where(low, jnp.int32(words[0]), jnp.int32(words[1])), sh) & 3

        return pick(0), pick(1), pick(2)

    def receives(w):
        return jnp.where(w == 0, zh, 1 - zh) == x

    def g_copy(u):
        return remote(give.at[u], got.at[u], g_send.at[u], g_recv.at[u], sibling)

    def x_copy(u, n, c):
        i = n * cands + c
        return remote(kept.at[u], xgot.at[i], x_send.at[i], x_recv.at[i], across)

    def o_ref(n, c, col):
        return out_hbm.at[pl.ds(pl.multiple_of(c * tok, tok), tok),
                          pl.ds(pl.multiple_of((col * NC + n) * cw, cw), cw)]

    def o_copy(u, n, c, zt):
        return remote(kept.at[u, pl.ds(zt * tok, tok)], o_ref(n, c, y),
                      o_send.at[zt, n * cands + c], o_recv.at[y, n * cands + c], out_target(zt))

    def o_local(u, n, c, zt):
        return pltpu.make_async_copy(kept.at[u, pl.ds(zt * tok, tok)], o_ref(n, c, y),
                                     o_send.at[zt, n * cands + c])

    def multiply(u):
        w, n, c = unit_of(u)

        def rows(i, _):
            r = pl.multiple_of(jnp.where(i == 0, 1 - core, core) * half, half)
            p = jnp.dot(attn[c, pl.ds(r, half)], wbuf[w, n],
                        preferred_element_type=F32).astype(BF16)

            @pl.when(i == 0)
            def _():
                give[u] = p
                g_copy(u).start()

            @pl.when(i == 1)
            def _():
                kept[u] = p
            return 0

        lax.fori_loop(0, 2, rows, 0)

    def pair(u):
        w, n, c = unit_of(u)

        @pl.when(jnp.logical_not(receives(w)))
        def _():
            g_copy(u).wait_recv()

            def block(b, _):
                r = pl.ds(pl.multiple_of(b * BLK, BLK), BLK)
                kept[u, r] = (kept[u, r].astype(F32) + got[u, r].astype(F32)).astype(BF16)
                return 0

            lax.fori_loop(0, half // BLK, block, 0)
            x_copy(u, n, c).start()

    def finish(u):
        w, n, c = unit_of(u)

        @pl.when(receives(w))
        def _():
            g_copy(u).wait_recv()
            i = n * cands + c
            x_copy(u, n, c).wait_recv()

            def block(b, _):
                r = pl.ds(pl.multiple_of(b * BLK, BLK), BLK)
                kept[u, r] = (kept[u, r].astype(F32) + got[u, r].astype(F32)
                              + xgot[i, r].astype(F32)).astype(BF16)
                return 0

            lax.fori_loop(0, half // BLK, block, 0)
            for zt in range(2):
                own = at_home & (zl == zt)

                @pl.when(own)
                def _():
                    o_local(u, n, c, zt).start()

                @pl.when(jnp.logical_not(own))
                def _():
                    o_copy(u, n, c, zt).start()

    done = 0

    def stretch(lo, hi, lag, flush):
        nonlocal done

        def step(u, _):
            multiply(u)

            @pl.when(u > lo)
            def _():
                pair(u - 1)

            @pl.when(u - lag >= done)
            def _():
                finish(u - lag)
            return 0

        def rest(u, _):
            finish(u)
            return 0

        lax.fori_loop(lo, hi, step, 0)
        pair(jnp.int32(hi - 1))
        done = max(done, hi - lag)
        if flush:
            lax.fori_loop(done, hi, rest, 0)
            done = hi

    def need_w(n):
        w_copy(n).wait_recv()

    marks = [0]
    for seg in ORDER:
        marks.append(marks[-1] + len(seg))
    need_attn(0)
    need_w(0)
    stretch(marks[0], marks[1], LAG, False)
    relay_rest(cands - 1)
    need_attn(1)
    need_w(1)
    stretch(marks[1], marks[2], LAG, True)
    need_w(2)
    stretch(marks[2], marks[3], LAG, False)
    need_attn(2)
    stretch(marks[3], marks[4], LAG, False)
    need_w(3)
    stretch(marks[4], marks[5], LAG, True)

    def arrived(i, _):
        n, c = i // cands, i % cands
        for col in range(2):
            @pl.when(jnp.logical_not(at_home & (col == y)))
            def _():
                remote(o_ref(n, c, col), o_ref(n, c, col), o_send.at[0, i], o_recv.at[col, i],
                       out_source(col)).wait_recv()
        return 0

    lax.fori_loop(0, NC * cands, arrived, 0)

    def drain(u, _):
        w, n, c = unit_of(u)
        g_copy(u).wait_send()

        @pl.when(receives(w))
        def _():
            for zt in range(2):
                own = at_home & (zl == zt)

                @pl.when(own)
                def _():
                    o_local(u, n, c, zt).wait()

                @pl.when(jnp.logical_not(own))
                def _():
                    o_copy(u, n, c, zt).wait_send()

        @pl.when(jnp.logical_not(receives(w)))
        def _():
            x_copy(u, n, c).wait_send()
        return 0

    lax.fori_loop(0, units, drain, 0)

    def drain_attn(i, _):
        a_copy(0, i, y, zl).wait_send()
        a_copy(1, i, y, zl).wait_send()
        a_copy(2, i, y, 1 - zl).wait_send()
        return 0

    lax.fori_loop(0, pieces, drain_attn, 0)
    for n in range(NC):
        w_copy(n).wait_send()

    def drain_kv(j, _):
        @pl.when(has_up)
        def _():
            kv_up_copy(j).wait_send()
        kv_mate_copy(j, y).wait_send()
        return 0

    lax.fori_loop(0, z + 1, drain_kv, 0)


def quad(nctx, ntp, cands, kvh, group, tok, rw, cols,
         queries, keys, values, out_weight, block_keep, basec, bases, offc, offs):
    heads = kvh * group
    cg = cands * kvh
    cw = cols // NC
    units = 2 * NC * cands
    hbm = pl.BlockSpec(memory_space=pl.ANY)
    vmem = pl.BlockSpec(memory_space=pltpu.VMEM)
    dma = pltpu.SemaphoreType.DMA
    return pl.pallas_call(
        functools.partial(quad_kernel, cands, kvh, group, tok),
        out_shape=jax.ShapeDtypeStruct((cands * tok, 2 * cols), BF16),
        in_specs=[hbm] * 4 + [pl.BlockSpec(memory_space=pltpu.SMEM)] + [vmem] * 4,
        out_specs=hbm,
        scratch_shapes=[
            pltpu.VMEM((heads, tok, DH), BF16),
            pltpu.VMEM((nctx, 2 * kvh, tok, DH), BF16),
            pltpu.VMEM((cg, nctx, tok, DH), BF16),
            pltpu.VMEM((kvh, nctx, DH, tok), BF16),
            pltpu.VMEM((nctx, tok, tok), F32),
            pltpu.VMEM((cands, 4 * tok, rw), BF16),
            pltpu.VMEM((2, NC, rw, cw), BF16),
            pltpu.VMEM((units, 2 * tok, cw), BF16),
            pltpu.VMEM((units, 2 * tok, cw), BF16),
            pltpu.VMEM((units, 2 * tok, cw), BF16),
            pltpu.VMEM((NC * cands, 2 * tok, cw), BF16),
            dma((heads,)), dma((2 * kvh,)), dma((nctx // 2,)), dma((nctx // 2,)), dma((nctx,)),
            dma((NC,)), dma((NC,)), dma((NC,)),
            dma((3, cg)), dma((3, cg)), dma((units,)), dma((units,)),
            dma((NC * cands,)), dma((NC * cands,)), dma((2, NC * cands)), dma((2, NC * cands)),
        ],
        compiler_params=pltpu.CompilerParams(
            collective_id=0, has_side_effects=True, vmem_limit_bytes=63 * 2**20),
        cost_estimate=pl.CostEstimate(
            flops=4 * nctx * tok * tok * heads * cands * DH + 4 * 4 * cands * tok * rw * cols,
            bytes_accessed=4 * rw * cols * 2,
            transcendentals=nctx * tok * tok * heads * cands),
        name="attend_project",
    )(queries, keys, values, out_weight, block_keep, basec, bases, offc, offs)


def body(nctx, ntp, queries, keys, values, block_keep, scale_pick, scale_table, out_weight):
    tok = queries.shape[0]
    kvh = keys.shape[1] // DH
    group = queries.shape[1] // (kvh * DH)
    cands = scale_pick.shape[0]
    kv_all = scale_pick.shape[1]
    table_rows = scale_table.shape[0]
    rw, cols = out_weight.shape
    nk = nctx // 2
    cw = cols // NC
    heads = kvh * group
    rows = cands * tok
    here = lax.axis_index("tp") * kvh + jnp.arange(kvh, dtype=jnp.int32)
    select = jnp.arange(kv_all, dtype=jnp.int32)[None, :] == here[:, None]
    picks = jnp.sum(jnp.where(select[None], scale_pick[:, None, :], 0), axis=-1)
    hit = picks[..., None] == jnp.arange(table_rows, dtype=jnp.int32)
    scales = jnp.sum(jnp.where(hit[..., None], scale_table[None, None], 0.0), axis=2)
    inv = 1.0 / THETA ** (jnp.arange(DH // 2, dtype=F32) * 2.0 / DH)
    freq = (inv / scales).reshape(cands * kvh, 1, DH // 2)

    def table(positions):
        angle = positions.astype(F32)[None, :, None] * freq
        c, s = jnp.cos(angle), jnp.sin(angle)
        return jnp.concatenate([c, c], -1), jnp.concatenate([-s, s], -1)

    basec, bases = table(jnp.arange(tok, dtype=jnp.int32))
    offc, offs = table(jnp.arange(nctx, dtype=jnp.int32) * tok)
    cg = cands * kvh
    hbm = pl.BlockSpec(memory_space=pl.ANY)
    vmem = pl.BlockSpec(memory_space=pltpu.VMEM)
    dma = pltpu.SemaphoreType.DMA
    if quad_fits(nctx, ntp, cands, cols):
        out = quad(nctx, ntp, cands, kvh, group, tok, rw, cols,
                   queries, keys, values, out_weight, block_keep, basec, bases, offc, offs)
        return out.reshape(cands, tok, 2 * cols)
    flops = 4 * nctx * tok * tok * heads * cands * DH + 4 * rows * rw * cols * nk
    out = pl.pallas_call(
        functools.partial(chain_kernel, nctx, ntp, cands, kvh, group, tok),
        out_shape=jax.ShapeDtypeStruct((rows, 2 * cols), BF16),
        in_specs=[hbm] * 4 + [pl.BlockSpec(memory_space=pltpu.SMEM)] + [vmem] * 4,
        out_specs=hbm,
        scratch_shapes=[
            pltpu.VMEM((heads, tok, DH), BF16),
            pltpu.VMEM((nctx, 2 * kvh, tok, DH), BF16),
            pltpu.VMEM((cg, nctx, tok, DH), BF16),
            pltpu.VMEM((kvh, nctx, DH, tok), BF16),
            pltpu.VMEM((nctx, tok, tok), F32),
            pltpu.VMEM((2, rows, rw), BF16),
            pltpu.VMEM((nk, NC, rw, cw), BF16),
            pltpu.VMEM((nk - 1, NC, 2, rows, cw), BF16),
            pltpu.VMEM((ntp, NC, 2, rows, cw), BF16),
            pltpu.VMEM((2, NC, rows, cw), BF16),
            pltpu.VMEM((NC, rows, cw), BF16),
            dma((heads,)), dma((2 * kvh,)), dma((nk,)), dma((nk,)), dma((nctx,)),
            dma((NC,)), dma((2, nk * NC)), dma((nk * NC,)),
            dma((cands,)), dma((cands,)), dma((nk, NC)), dma((ntp, NC)),
            dma((NC,)), dma((NC,)), dma((2, NC)),
        ],
        compiler_params=pltpu.CompilerParams(
            collective_id=0, has_side_effects=True, vmem_limit_bytes=63 * 2**20),
        cost_estimate=pl.CostEstimate(
            flops=flops, bytes_accessed=4 * rw * cols * nk,
            transcendentals=nctx * tok * tok * heads * cands),
        name="attend_project",
    )(queries, keys, values, out_weight, block_keep, basec, bases, offc, offs)
    return out.reshape(cands, tok, 2 * cols)


def solution(mesh):
    return jax.shard_map(
        functools.partial(body, mesh.shape["ctx"], mesh.shape["tp"]),
        mesh=mesh,
        in_specs=(P("ctx", "tp"), P("ctx", "tp"), P("ctx", "tp"), P(), P(), P(), P("tp", "ctx")),
        out_specs=P(None, "ctx", "tp"),
        check_vma=False,
    )
```

```python
import functools
import math

import jax
import jax.numpy as jnp
from jax import lax
from jax.experimental import pallas as pl
from jax.experimental.pallas import tpu as pltpu
from jax.sharding import PartitionSpec as P

DH = 128
BLK = 128
NC = 4
THETA = 500000.0
LOW = -1e30
MESH = pl.DeviceIdType.MESH
F32 = jnp.float32
BF16 = jnp.bfloat16


def chain_kernel(nctx, ntp, cands, kvh, group, tok,
           q_hbm, k_hbm, v_hbm, w_hbm, keep_ref, basec, bases, offc, offs,
           out_hbm,
           qv, kv, krot, vt, bias, attn, wbuf, pbuf, rbuf, obuf, ybuf,
           q_sem, kv_sem, kv_up, kv_y, kv_recv, w_local, w_send, w_recv,
           a_send, a_recv, p_send, p_recv, y_send, y_recv, o_sem):
    nk = nctx // 2
    me = lax.axis_index("ctx")
    t = lax.axis_index("tp")
    k = me // 2
    y = me % 2
    other = 1 - y
    cw = wbuf.shape[3]
    rows = cands * tok
    heads = kvh * group
    has_up = k + 1 < nk
    has_down = k > 0
    mate = (me + 1 - 2 * y, t)
    up = (jnp.minimum(k + 1, nk - 1) * 2 + y, t)
    down = (jnp.maximum(k - 1, 0) * 2 + y, t)

    def remote(src, dst, ssem, rsem, dev):
        return pltpu.make_async_remote_copy(
            src_ref=src, dst_ref=dst, send_sem=ssem, recv_sem=rsem,
            device_id=dev, device_id_type=MESH)

    q_copies = [
        pltpu.make_async_copy(q_hbm.at[:, pl.ds(h * DH, DH)], qv.at[h], q_sem.at[h])
        for h in range(heads)
    ]
    kv_copies = [
        pltpu.make_async_copy(src.at[:, pl.ds(g * DH, DH)], kv.at[me, i * kvh + g],
                              kv_sem.at[i * kvh + g])
        for i, src in enumerate((k_hbm, v_hbm)) for g in range(kvh)
    ]
    w_copies = [
        pltpu.make_async_copy(w_hbm.at[:, pl.ds(n * cw, cw)], wbuf.at[k, n], w_local.at[n])
        for n in range(NC)
    ]
    for c in kv_copies + q_copies:
        c.start()

    bar = pltpu.get_barrier_semaphore()
    pl.semaphore_signal(bar, inc=1, device_id=mate, device_id_type=MESH)
    for d in range(1, ntp):
        pl.semaphore_signal(bar, inc=1, device_id=(me, lax.rem(t + d, ntp)), device_id_type=MESH)

    @pl.when(has_up)
    def _():
        pl.semaphore_signal(bar, inc=1, device_id=up, device_id_type=MESH)

    @pl.when(has_down)
    def _():
        pl.semaphore_signal(bar, inc=1, device_id=down, device_id_type=MESH)

    pl.semaphore_wait(bar, ntp + has_up.astype(jnp.int32) + has_down.astype(jnp.int32))

    def kv_up_copy(j):
        s = 2 * j + y
        return remote(kv.at[s], kv.at[s], kv_up.at[j], kv_recv.at[s], up)

    def kv_mate_copy(j, col):
        s = 2 * j + col
        return remote(kv.at[s], kv.at[s], kv_y.at[j], kv_recv.at[s], mate)

    def kv_pass(j):
        @pl.when(has_up)
        def _():
            kv_up_copy(j).start()
        kv_mate_copy(j, y).start()

    def w_up_copy(j, n, src=None):
        return remote(wbuf.at[j, n] if src is None else src, wbuf.at[j, n],
                      w_send.at[0, j * NC + n], w_recv.at[j * NC + n], up)

    def w_down_copy(j, n, src=None):
        return remote(wbuf.at[j, n] if src is None else src, wbuf.at[j, n],
                      w_send.at[1, j * NC + n], w_recv.at[j * NC + n], down)

    for c in kv_copies:
        c.wait()
    kv_pass(k)
    @pl.when(has_down)
    def _():
        for n in range(NC):
            w_down_copy(k, n, w_hbm.at[:, pl.ds(n * cw, cw)]).start()
    for c in w_copies:
        c.start()

    kio = lax.broadcasted_iota(jnp.int32, (tok, tok), 0)
    qio = lax.broadcasted_iota(jnp.int32, (tok, tok), 1)
    nb = tok // BLK

    def make_bias(j, _):
        seen = jnp.zeros((tok, tok), jnp.int32)
        for a in range(nb):
            for b in range(nb):
                here = (qio // BLK == a) & (kio // BLK == b)
                seen = jnp.where(here, keep_ref[me * nb + a, j * nb + b], seen)
        ok = (seen == 1) & (kio + (j - me) * tok <= qio)
        bias[j] = jnp.where(ok, 0.0, LOW)
        return 0

    def tables(cg, j):
        bc, bs = basec[cg], bases[cg]
        oc = offc[cg, pl.ds(j, 1)]
        os = offs[cg, pl.ds(j, 1)]
        return bc * oc - bs * os, bs * oc + bc * os

    def turn(x, c, s):
        x = x.astype(F32)
        return (x * c + pltpu.roll(x, DH // 2, 1) * s).astype(BF16)

    for s in range(1, nk):
        @pl.when(k >= s)
        def _():
            kv_up_copy(k - s).wait_recv()
            kv_pass(k - s)

    @pl.when(has_up)
    def _():
        for n in range(NC):
            w_up_copy(k, n, w_hbm.at[:, pl.ds(n * cw, cw)]).start()

    def from_mate(j, _):
        kv_mate_copy(j, other).wait_recv()
        return 0

    lax.fori_loop(0, me + 1, make_bias, 0)
    lax.fori_loop(0, k + 1, from_mate, 0)

    def prepare(j, _):
        for g in range(kvh):
            vt[g, j] = jnp.transpose(kv[j, kvh + g].astype(F32)).astype(BF16)
            x = kv[j, g]
            for c in range(cands):
                cc, ss = tables(c * kvh + g, j)
                krot[c * kvh + g, j] = turn(x, cc, ss)
        return 0

    lax.fori_loop(0, me + 1, prepare, 0)
    for c in q_copies:
        c.wait()

    def forward(s, n):
        @pl.when((k >= s) & has_up)
        def _():
            w_up_copy(k - s, n).wait_recv()
            w_up_copy(k - s, n).start()

        @pl.when((k + s < nk) & has_down)
        def _():
            w_down_copy(k + s, n).wait_recv()
            w_down_copy(k + s, n).start()

    wide = 4
    per_c = kvh * group // wide
    c2 = DH ** (-0.5) * math.log2(math.e)

    def attn_copy(c, col):
        part = attn.at[col, pl.ds(c * tok, tok)]
        return remote(part, part, a_send.at[c], a_recv.at[c], mate)

    def candidate(c, _):
        def unit(i, _):
            g = i // (group // wide)
            cg = c * kvh + g
            h0 = wide * i
            cc, ss = tables(cg, me)
            qr = [turn(qv[h0 + d], cc, ss) for d in range(wide)]

            def step(j, state):
                kt = krot[cg, j]
                vv = vt[g, j]
                bj = bias[j]
                new = []
                sts = [lax.dot_general(kt, qr[d], (((1,), (1,)), ((), ())),
                                       preferred_element_type=F32) + bj
                       for d in range(wide)]
                for d in range(wide):
                    m, l, acc = state[d]
                    st = sts[d]
                    mn = jnp.maximum(m, jnp.max(st, axis=0, keepdims=True))
                    p = jnp.exp2((st - mn) * c2)
                    al = jnp.exp2((m - mn) * c2)
                    l = l * al + jnp.sum(p, axis=0, keepdims=True)
                    acc = acc * al + jnp.dot(vv, p.astype(BF16), preferred_element_type=F32)
                    new.append((mn, l, acc))
                return tuple(new)

            one = (jnp.full((1, tok), LOW, F32), jnp.zeros((1, tok), F32),
                   jnp.zeros((DH, tok), F32))
            state = lax.fori_loop(0, me + 1, step, (one,) * wide)
            for d in range(wide):
                m, l, acc = state[d]
                at = pl.multiple_of((h0 + d) * DH, DH)
                attn[y, pl.ds(pl.multiple_of(c * tok, tok), tok), pl.ds(at, DH)] = (
                    jnp.transpose(acc / l).astype(BF16))
            return 0

        lax.fori_loop(0, per_c, unit, 0)
        attn_copy(c, y).start()
        return 0

    lax.fori_loop(0, cands, candidate, 0)
    for c in w_copies:
        c.wait()
    for c in range(cands):
        attn_copy(c, other).wait_recv()

    def slot(j):
        return jnp.minimum(j - (j > t).astype(jnp.int32), nk - 2)

    def p_copy(j, n):
        return remote(pbuf.at[slot(j), n], rbuf.at[t, n], p_send.at[j, n], p_recv.at[t, n], (me, j))

    def p_arrive(src, n):
        return remote(rbuf.at[src, n], rbuf.at[src, n], p_send.at[src, n], p_recv.at[src, n],
                      (me, src))

    def y_copy(n, col):
        return remote(ybuf.at[n], obuf.at[col, n], y_send.at[n], y_recv.at[n], mate)

    def o_copy(col, n):
        return pltpu.make_async_copy(
            obuf.at[col, n],
            out_hbm.at[:, pl.ds(pl.multiple_of((col * NC + n) * cw, cw), cw)],
            o_sem.at[col, n])

    def project(j, n, dest):
        def block(half, _):
            dest[half] = jnp.dot(
                attn[half], wbuf[j, n], preferred_element_type=F32).astype(BF16)
            return 0
        lax.fori_loop(0, 2, block, 0)

    def compute(p, d, n):
        j = k - p if d == 0 else k + p
        ok = k >= p if d == 0 else k + p < nk
        fwd = has_up if d == 0 else has_down
        if p > 0:
            @pl.when(ok & jnp.logical_not(fwd))
            def _():
                (w_up_copy if d == 0 else w_down_copy)(j, n).wait_recv()
        @pl.when(ok & (j != t))
        def _():
            project(j, n, pbuf.at[slot(j), n])
            p_copy(j, n).start()

        @pl.when(ok & (j == t))
        def _():
            project(j, n, rbuf.at[t, n])

    def finish(n):
        for d in range(1, ntp):
            p_arrive(lax.rem(t + d, ntp), n).wait_recv()

        def total(half, r):
            acc = rbuf[0, n, half, pl.ds(r, BLK)].astype(F32)
            for src in range(1, ntp):
                acc = acc + rbuf[src, n, half, pl.ds(r, BLK)].astype(F32)
            return acc.astype(BF16)

        def block(b, _):
            r = pl.multiple_of(b * BLK, BLK)
            ybuf[n, pl.ds(r, BLK)] = total(other, r)
            return 0

        lax.fori_loop(0, rows // BLK, block, 0)
        y_copy(n, y).start()

        def block2(b, _):
            r = pl.multiple_of(b * BLK, BLK)
            obuf[y, n, pl.ds(r, BLK)] = total(y, r)
            return 0

        lax.fori_loop(0, rows // BLK, block2, 0)
        o_copy(y, n).start()

    for p in range(nk):
        mine = (t == k - p) | (t == k + p)

        if 0 < p < nk - 1:
            def pass_on(n, _):
                forward(p, n)
                return 0
            lax.fori_loop(0, NC, pass_on, 0)

        def chunk(n, _):
            compute(p, 0, n)
            if p > 0:
                compute(p, 1, n)

            @pl.when(mine & (n > 0))
            def _():
                finish(n - 1)
            return 0

        lax.fori_loop(0, NC, chunk, 0)

        @pl.when(mine)
        def _():
            finish(NC - 1)

    def drain(n, _):
        y_copy(n, other).wait_recv()
        o_copy(other, n).start()
        return 0

    lax.fori_loop(0, NC, drain, 0)

    def drain2(n, _):
        def sent(j, _):
            @pl.when(j != t)
            def _():
                p_copy(j, n).wait_send()
            return 0
        lax.fori_loop(0, nk, sent, 0)
        y_copy(n, y).wait_send()
        o_copy(y, n).wait()
        o_copy(other, n).wait()
        return 0

    lax.fori_loop(0, NC, drain2, 0)
    for c in range(cands):
        attn_copy(c, y).wait_send()

    def drain_kv(j, _):
        @pl.when(has_up)
        def _():
            kv_up_copy(j).wait_send()

            def each(n, _):
                w_up_copy(j, n).wait_send()
                return 0
            lax.fori_loop(0, NC, each, 0)
        kv_mate_copy(j, y).wait_send()
        return 0

    lax.fori_loop(0, k + 1, drain_kv, 0)

    @pl.when(has_down)
    def _():
        def drain_down(j, _):
            def each(n, _):
                w_down_copy(j, n).wait_send()
                return 0
            lax.fori_loop(0, NC, each, 0)
            return 0
        lax.fori_loop(k, nk, drain_down, 0)


ISSUE = (
    (0, 0, 0, 0),
    (1, 1, 1, 1),
    (0, 0, 0, 0),
    (0, 0, 0, 0),
)
LAG = 8
ORDER = (
    ((0, 0, 0, 0), (1, 0, 0, 0), (0, 1, 0, 0), (0, 2, 0, 0), (0, 3, 0, 0),
     (0, 0, 1, 0), (1, 0, 1, 0), (0, 1, 1, 0), (1, 0, 2, 0), (0, 2, 1, 0), (1, 1, 0, 0),
     (0, 3, 1, 0), (1, 1, 1, 0), (0, 0, 2, 0), (1, 1, 2, 0), (0, 1, 2, 0), (0, 2, 2, 0),
     (0, 3, 2, 0)),
    ((0, 0, 0, 1), (1, 0, 0, 1), (0, 1, 0, 1), (1, 1, 0, 1), (0, 2, 0, 1), (0, 3, 0, 1)),
    ((1, 2, 0, 0), (1, 2, 1, 0), (1, 2, 2, 0), (1, 2, 0, 1)),
    ((0, 0, 1, 1), (1, 0, 1, 1), (0, 1, 1, 1), (1, 1, 1, 1), (0, 2, 1, 1), (1, 2, 1, 1),
     (0, 3, 1, 1)),
    ((0, 0, 2, 1), (1, 0, 2, 1), (0, 1, 2, 1), (1, 1, 2, 1), (0, 2, 2, 1), (1, 2, 2, 1),
     (0, 3, 2, 1)),
    ((1, 3, 0, 0), (1, 3, 1, 0), (1, 3, 2, 0), (1, 3, 0, 1), (1, 3, 1, 1), (1, 3, 2, 1)),
)
NEEDS = (((), (0, 1), False), ((0,), (), True), ((), (2,), False), ((1,), (), True),
         ((2,), (), False), ((), (3,), True))


def quad_fits(nctx, ntp, cands, cols):
    return nctx == 8 and ntp == 4 and cands == 3 and cols % (NC * DH) == 0


def quad_kernel(cands, kvh, group, tok,
                q_hbm, k_hbm, v_hbm, w_hbm, keep_ref, basec, bases, offc, offs,
                out_hbm,
                qv, kv, krot, vt, bias, attn, wbuf, give, kept, got, xgot,
                q_sem, kv_sem, kv_up, kv_y, kv_near, kv_recv, w_local, w_send, w_recv,
                a_send, a_recv, g_send, g_recv, x_send, x_recv, o_send, o_recv):
    nz = 4
    me = lax.axis_index("ctx")
    t = lax.axis_index("tp")
    z, y = me // 2, me % 2
    zh, zl = z // 2, z % 2
    x, core = t // 2, t % 2
    cw = wbuf.shape[3]
    heads = kvh * group
    half = 2 * tok
    width = group * DH
    has_up = z + 1 < nz
    has_down = z > 0
    one = jnp.int32(1)

    mate = (z * 2 + 1 - y, t)
    up = (jnp.minimum(z + 1, nz - 1) * 2 + y, t)
    down = (jnp.maximum(z - 1, 0) * 2 + y, t)
    near = ((zh * 2 + 1 - zl) * 2 + y, t)
    far = (((1 - zh) * 2 + zl) * 2 + y, t)
    sibling = (me, x * 2 + 1 - core)
    across = (me, (1 - x) * 2 + core)
    at_home = (zl == core) & (core == y)

    def remote(src, dst, ssem, rsem, dev):
        return pltpu.make_async_remote_copy(
            src_ref=src, dst_ref=dst, send_sem=ssem, recv_sem=rsem,
            device_id=dev, device_id_type=MESH)

    q_local = pltpu.make_async_copy(q_hbm, qv.at[zl], q_sem.at[0])
    q_near = remote(q_hbm, qv.at[zl], q_sem.at[1], q_sem.at[2], near)
    q_from = remote(q_hbm, qv.at[1 - zl], q_sem.at[1], q_sem.at[2], near)
    kv_copies = [
        pltpu.make_async_copy(src.at[:, pl.ds(g * DH, DH)], kv.at[me, i * kvh + g],
                              kv_sem.at[i * kvh + g])
        for i, src in enumerate((k_hbm, v_hbm)) for g in range(kvh)
    ]
    w_copies = [
        pltpu.make_async_copy(w_hbm.at[:, pl.ds(n * cw, cw)], wbuf.at[0, n], w_local.at[n])
        for n in range(NC)
    ]
    for c in kv_copies + [q_local]:
        c.start()

    def out_target(zt):
        return ((zh * 2 + zt) * 2 + core, x * 2 + zl)

    def out_source(col):
        return ((zh * 2 + core) * 2 + col, x * 2 + y)

    bar = pltpu.get_barrier_semaphore()
    for dev in (mate, near, far, sibling, across):
        pl.semaphore_signal(bar, inc=1, device_id=dev, device_id_type=MESH)

    @pl.when(has_down)
    def _():
        pl.semaphore_signal(bar, inc=1, device_id=down, device_id_type=MESH)

    for col in range(2):
        @pl.when(jnp.logical_not(at_home & (col == y)))
        def _():
            pl.semaphore_signal(bar, inc=1, device_id=out_source(col), device_id_type=MESH)

    pl.semaphore_wait(bar, 7 + has_up.astype(jnp.int32) - at_home.astype(jnp.int32))

    def kv_up_copy(j):
        s = 2 * j + y
        return remote(kv.at[s], kv.at[s], kv_up.at[j], kv_recv.at[s], up)

    def kv_mate_copy(j, col):
        s = 2 * j + col
        return remote(kv.at[s], kv.at[s], kv_y.at[j], kv_recv.at[s], mate)

    def kv_pass(j):
        @pl.when(has_up)
        def _():
            kv_up_copy(j).start()
        kv_mate_copy(j, y).start()

    def kv_near_copy(zz):
        s = 2 * zz + y
        return remote(kv.at[s], kv.at[s], kv_near.at[0], kv_recv.at[s], near)

    def w_copy(n):
        return remote(w_hbm.at[:, pl.ds(n * cw, cw)], wbuf.at[1, n],
                      w_send.at[n], w_recv.at[n], far)

    def issue(point):
        for zz in range(nz):
            for n in range(NC):
                if ISSUE[zz][n] in (point if isinstance(point, range) else (point,)):
                    here = z == zz

                    @pl.when(here)
                    def _():
                        w_copy(n).start()

    for c in kv_copies:
        c.wait()
    kv_pass(z)

    @pl.when(zl == 1)
    def _():
        kv_near_copy(z).start()
        q_near.start()

    @pl.when(z == 0)
    def _():
        q_near.start()

    issue(0)
    for c in w_copies:
        c.start()

    top = (zh * 2 + 1) * 2 + y
    blocks = bias.shape[1]
    kio = lax.broadcasted_iota(jnp.int32, (tok, tok), 0)
    qio = lax.broadcasted_iota(jnp.int32, (tok, tok), 1)
    nb = tok // BLK

    def make_bias(i, _):
        zt, j = i // blocks, i % blocks
        mine = (zh * 2 + zt) * 2 + y
        seen = jnp.zeros((tok, tok), jnp.int32)
        for a in range(nb):
            for b in range(nb):
                here = (qio // BLK == a) & (kio // BLK == b)
                seen = jnp.where(here, keep_ref[mine * nb + a, j * nb + b], seen)
        ok = (seen == 1) & (kio + (j - mine) * tok <= qio)
        bias[zt, j] = jnp.where(ok, 0.0, LOW)
        return 0

    def tables(cg, j):
        bc, bs = basec[cg], bases[cg]
        oc = offc[cg, pl.ds(j, 1)]
        os = offs[cg, pl.ds(j, 1)]
        return bc * oc - bs * os, bs * oc + bc * os

    def turn(v, c, s):
        v = v.astype(F32)
        return (v * c + pltpu.roll(v, DH // 2, 1) * s).astype(BF16)

    def prepare(zz):
        kv_mate_copy(zz, 1 - y).wait_recv()

        def block(j, _):
            for g in range(kvh):
                vt[g, j] = jnp.transpose(kv[j, kvh + g].astype(F32)).astype(BF16)
                v = kv[j, g]
                for c in range(cands):
                    cc, ss = tables(c * kvh + g, j)
                    krot[c * kvh + g, j] = turn(v, cc, ss)
            return 0

        lax.fori_loop(2 * zz, 2 * zz + 2, block, 0)

    lax.fori_loop(0, 2 * blocks, make_bias, 0)

    def fetch(s, _):
        kv_up_copy(z - s).wait_recv()
        kv_pass(z - s)
        prepare(z - s + 1)
        return 0

    lax.fori_loop(1, z + 1, fetch, 0)

    @pl.when(zl == 0)
    def _():
        @pl.when(z > 0)
        def _():
            q_near.start()
        kv_near_copy(z + 1).wait_recv()
        kv_mate_copy(z + 1, y).start()

    issue(1)
    prepare(jnp.int32(0))

    @pl.when(zl == 0)
    def _():
        prepare(z + 1)

    q_local.wait()
    q_from.wait_recv()

    pieces = cands * kvh
    c2 = DH ** (-0.5) * math.log2(math.e)

    def a_copy(i, ty, zt):
        c, g = i // kvh, i % kvh
        p = attn.at[c, pl.ds(pl.multiple_of((ty * 2 + zt) * tok, tok), tok),
                    pl.ds(pl.multiple_of(g * width, width), width)]
        return remote(p, p, a_send.at[zt, i], a_recv.at[zt, i], mate)

    def attend(i, zt):
        c, g = i // kvh, i % kvh
        mine = (zh * 2 + zt) * 2 + y
        cc, ss = tables(i, mine)
        cc, ss = cc * c2, ss * c2
        qr = [turn(qv[zt, :, pl.ds(pl.multiple_of((g * group + d) * DH, DH), DH)], cc, ss)
              for d in range(group)]

        def step(j, state):
            js = [2 * j, jnp.minimum(2 * j + 1, top)]
            bs = [bias[zt, 2 * j], bias[zt, 2 * j + 1]]
            new = []
            sts = [[lax.dot_general(krot[i, jj], qr[d], (((1,), (1,)), ((), ())),
                                    preferred_element_type=F32) + bj
                    for jj, bj in zip(js, bs)] for d in range(group)]
            for d in range(group):
                m, l, acc = state[d]
                mn = m
                for st in sts[d]:
                    mn = jnp.maximum(mn, jnp.max(st, axis=0, keepdims=True))
                al = jnp.exp2(m - mn)
                l, acc = l * al, acc * al
                for jj, st in zip(js, sts[d]):
                    p = jnp.exp2(st - mn)
                    l = l + jnp.sum(p, axis=0, keepdims=True)
                    acc = acc + jnp.dot(vt[g, jj], p.astype(BF16), preferred_element_type=F32)
                new.append((mn, l, acc))
            return tuple(new)

        first = (jnp.full((1, tok), LOW, F32), jnp.zeros((1, tok), F32),
                 jnp.zeros((DH, tok), F32))
        state = lax.fori_loop(0, mine // 2 + 1, step, (first,) * group)
        for d in range(group):
            m, l, acc = state[d]
            at = pl.multiple_of((g * group + d) * DH, DH)
            attn[c, pl.ds(pl.multiple_of((y * 2 + zt) * tok, tok), tok), pl.ds(at, DH)] = (
                jnp.transpose(acc / l).astype(BF16))

    def piece(i, _):
        def both(k, _):
            zt = zl + k * (1 - 2 * zl)
            attend(i, zt)
            a_copy(i, y, zt).start()
            return 0

        lax.fori_loop(0, 2, both, 0)
        for zz in range(nz):
            for n in range(NC):
                if 2 <= ISSUE[zz][n] < 2 + pieces:
                    @pl.when((z == zz) & (i == ISSUE[zz][n] - 2))
                    def _():
                        w_copy(n).start()
        return 0

    lax.fori_loop(0, pieces, piece, 0)
    issue(2 + pieces)
    for c in w_copies:
        c.wait()

    def need_attn(c):
        for g in range(kvh):
            for zt in range(2):
                a_copy(c * kvh + g, 1 - y, zt).wait_recv()

    table = [v for seg in ORDER for v in seg]

    def unit_of(u):
        block = u // 12
        sh = 2 * (u % 12)

        def pick(k):
            word = jnp.int32(0)
            for b in range(0, len(table), 12):
                bits = sum(v[k] << (2 * i) for i, v in enumerate(table[b:b + 12]))
                word = jnp.where(block == b // 12, jnp.int32(bits), word)
            return lax.shift_right_logical(word, sh) & 3

        return pick(0), pick(1), pick(2), pick(3)

    def receives(w):
        return jnp.where(w == 0, zh, 1 - zh) == x

    def g_copy(u):
        return remote(give.at[u], got.at[u], g_send.at[u], g_recv.at[u], sibling)

    def x_copy(u, n, c):
        i = n * cands + c
        return remote(kept.at[u], xgot.at[i], x_send.at[i], x_recv.at[i], across)

    def o_ref(n, c, col):
        return out_hbm.at[pl.ds(pl.multiple_of(c * tok, tok), tok),
                          pl.ds(pl.multiple_of((col * NC + n) * cw, cw), cw)]

    def o_copy(u, n, c, zt):
        return remote(kept.at[u, pl.ds(zt * tok, tok)], o_ref(n, c, y),
                      o_send.at[zt, n * cands + c], o_recv.at[y, n * cands + c], out_target(zt))

    def o_local(u, n, c, zt):
        return pltpu.make_async_copy(kept.at[u, pl.ds(zt * tok, tok)], o_ref(n, c, y),
                                     o_send.at[zt, n * cands + c])

    def slot(w, n, c):
        return (w * NC + n) * cands + c

    def reduces(h):
        return (h == 0) == (core == y)

    def multiply(u):
        w, n, c, h = unit_of(u)
        i = slot(w, n, c)
        r = pl.multiple_of(jnp.where(h == 0, y, 1 - y) * half, half)
        p = jnp.dot(attn[c, pl.ds(r, half)], wbuf[w, n], preferred_element_type=F32).astype(BF16)

        @pl.when(reduces(h))
        def _():
            kept[i] = p

        @pl.when(jnp.logical_not(reduces(h)))
        def _():
            give[i] = p
            g_copy(i).start()

    def pair(u):
        w, n, c, h = unit_of(u)
        i = slot(w, n, c)

        @pl.when(reduces(h) & jnp.logical_not(receives(w)))
        def _():
            g_copy(i).wait_recv()

            def block(b, _):
                r = pl.ds(pl.multiple_of(b * BLK, BLK), BLK)
                kept[i, r] = (kept[i, r].astype(F32) + got[i, r].astype(F32)).astype(BF16)
                return 0

            lax.fori_loop(0, half // BLK, block, 0)
            x_copy(i, n, c).start()

    def finish(u):
        w, n, c, h = unit_of(u)
        i = slot(w, n, c)

        @pl.when(reduces(h) & receives(w))
        def _():
            g_copy(i).wait_recv()
            x_copy(i, n, c).wait_recv()

            def block(b, _):
                r = pl.ds(pl.multiple_of(b * BLK, BLK), BLK)
                kept[i, r] = (kept[i, r].astype(F32) + got[i, r].astype(F32)
                              + xgot[n * cands + c, r].astype(F32)).astype(BF16)
                return 0

            lax.fori_loop(0, half // BLK, block, 0)
            for zt in range(2):
                own = at_home & (zl == zt)

                @pl.when(own)
                def _():
                    o_local(i, n, c, zt).start()

                @pl.when(jnp.logical_not(own))
                def _():
                    o_copy(i, n, c, zt).start()

    done = 0

    def stretch(lo, hi, lag, flush):
        nonlocal done

        def step(u, _):
            multiply(u)

            @pl.when(u > lo)
            def _():
                pair(u - 1)

            @pl.when(u - lag >= done)
            def _():
                finish(u - lag)
            return 0

        def rest(u, _):
            finish(u)
            return 0

        lax.fori_loop(lo, hi, step, 0)
        pair(jnp.int32(hi - 1))
        done = max(done, hi - lag)
        if flush:
            lax.fori_loop(done, hi, rest, 0)
            done = hi

    def need_w(n):
        w_copy(n).wait_recv()

    marks = [0]
    for seg in ORDER:
        marks.append(marks[-1] + len(seg))
    for seg, (attn_of, w_of, flush) in enumerate(NEEDS):
        for c in attn_of:
            need_attn(c)
        for n in w_of:
            need_w(n)
        stretch(marks[seg], marks[seg + 1], LAG, flush)
        issue(3 + pieces + seg)

    def arrived(i, _):
        n, c = i // cands, i % cands
        for col in range(2):
            @pl.when(jnp.logical_not(at_home & (col == y)))
            def _():
                remote(o_ref(n, c, col), o_ref(n, c, col), o_send.at[0, i], o_recv.at[col, i],
                       out_source(col)).wait_recv()
        return 0

    lax.fori_loop(0, NC * cands, arrived, 0)

    def drain(u, _):
        w, n, c = u // (NC * cands), (u // cands) % NC, u % cands
        g_copy(u).wait_send()

        @pl.when(receives(w))
        def _():
            for zt in range(2):
                own = at_home & (zl == zt)

                @pl.when(own)
                def _():
                    o_local(u, n, c, zt).wait()

                @pl.when(jnp.logical_not(own))
                def _():
                    o_copy(u, n, c, zt).wait_send()

        @pl.when(jnp.logical_not(receives(w)))
        def _():
            x_copy(u, n, c).wait_send()
        return 0

    lax.fori_loop(0, 2 * NC * cands, drain, 0)

    def drain_attn(i, _):
        for zt in range(2):
            a_copy(i, y, zt).wait_send()
        return 0

    lax.fori_loop(0, pieces, drain_attn, 0)
    for n in range(NC):
        w_copy(n).wait_send()

    q_near.wait_send()

    @pl.when(zl == 1)
    def _():
        kv_near_copy(z).wait_send()

    @pl.when(zl == 0)
    def _():
        kv_mate_copy(z + 1, y).wait_send()

    def drain_kv(j, _):
        @pl.when(has_up)
        def _():
            kv_up_copy(j).wait_send()
        kv_mate_copy(j, y).wait_send()
        return 0

    lax.fori_loop(0, z + 1, drain_kv, 0)


def quad(nctx, ntp, cands, kvh, group, tok, rw, cols,
         queries, keys, values, out_weight, block_keep, basec, bases, offc, offs):
    heads = kvh * group
    cg = cands * kvh
    cw = cols // NC
    units = 2 * NC * cands
    hbm = pl.BlockSpec(memory_space=pl.ANY)
    vmem = pl.BlockSpec(memory_space=pltpu.VMEM)
    dma = pltpu.SemaphoreType.DMA
    return pl.pallas_call(
        functools.partial(quad_kernel, cands, kvh, group, tok),
        out_shape=jax.ShapeDtypeStruct((cands * tok, 2 * cols), BF16),
        in_specs=[hbm] * 4 + [pl.BlockSpec(memory_space=pltpu.SMEM)] + [vmem] * 4,
        out_specs=hbm,
        scratch_shapes=[
            pltpu.VMEM((2, tok, heads * DH), BF16),
            pltpu.VMEM((nctx, 2 * kvh, tok, DH), BF16),
            pltpu.VMEM((cg, nctx, tok, DH), BF16),
            pltpu.VMEM((kvh, nctx, DH, tok), BF16),
            pltpu.VMEM((2, nctx, tok, tok), F32),
            pltpu.VMEM((cands, 4 * tok, rw), BF16),
            pltpu.VMEM((2, NC, rw, cw), BF16),
            pltpu.VMEM((units, 2 * tok, cw), BF16),
            pltpu.VMEM((units, 2 * tok, cw), BF16),
            pltpu.VMEM((units, 2 * tok, cw), BF16),
            pltpu.VMEM((NC * cands, 2 * tok, cw), BF16),
            dma((3,)), dma((2 * kvh,)), dma((nctx // 2,)), dma((nctx // 2,)), dma((1,)), dma((nctx,)),
            dma((NC,)), dma((NC,)), dma((NC,)),
            dma((2, cg)), dma((2, cg)), dma((units,)), dma((units,)),
            dma((NC * cands,)), dma((NC * cands,)), dma((2, NC * cands)), dma((2, NC * cands)),
        ],
        compiler_params=pltpu.CompilerParams(
            collective_id=0, has_side_effects=True, vmem_limit_bytes=63 * 2**20),
        cost_estimate=pl.CostEstimate(
            flops=4 * nctx * tok * tok * heads * cands * DH + 4 * 4 * cands * tok * rw * cols,
            bytes_accessed=4 * rw * cols * 2,
            transcendentals=nctx * tok * tok * heads * cands),
        name="attend_project",
    )(queries, keys, values, out_weight, block_keep, basec, bases, offc, offs)


def body(nctx, ntp, queries, keys, values, block_keep, scale_pick, scale_table, out_weight):
    tok = queries.shape[0]
    kvh = keys.shape[1] // DH
    group = queries.shape[1] // (kvh * DH)
    cands = scale_pick.shape[0]
    kv_all = scale_pick.shape[1]
    table_rows = scale_table.shape[0]
    rw, cols = out_weight.shape
    nk = nctx // 2
    cw = cols // NC
    heads = kvh * group
    rows = cands * tok
    here = lax.axis_index("tp") * kvh + jnp.arange(kvh, dtype=jnp.int32)
    select = jnp.arange(kv_all, dtype=jnp.int32)[None, :] == here[:, None]
    picks = jnp.sum(jnp.where(select[None], scale_pick[:, None, :], 0), axis=-1)
    hit = picks[..., None] == jnp.arange(table_rows, dtype=jnp.int32)
    scales = jnp.sum(jnp.where(hit[..., None], scale_table[None, None], 0.0), axis=2)
    inv = 1.0 / THETA ** (jnp.arange(DH // 2, dtype=F32) * 2.0 / DH)
    freq = (inv / scales).reshape(cands * kvh, 1, DH // 2)

    def table(positions):
        angle = positions.astype(F32)[None, :, None] * freq
        c, s = jnp.cos(angle), jnp.sin(angle)
        return jnp.concatenate([c, c], -1), jnp.concatenate([-s, s], -1)

    basec, bases = table(jnp.arange(tok, dtype=jnp.int32))
    offc, offs = table(jnp.arange(nctx, dtype=jnp.int32) * tok)
    cg = cands * kvh
    hbm = pl.BlockSpec(memory_space=pl.ANY)
    vmem = pl.BlockSpec(memory_space=pltpu.VMEM)
    dma = pltpu.SemaphoreType.DMA
    if quad_fits(nctx, ntp, cands, cols):
        out = quad(nctx, ntp, cands, kvh, group, tok, rw, cols,
                   queries, keys, values, out_weight, block_keep, basec, bases, offc, offs)
        return out.reshape(cands, tok, 2 * cols)
    flops = 4 * nctx * tok * tok * heads * cands * DH + 4 * rows * rw * cols * nk
    out = pl.pallas_call(
        functools.partial(chain_kernel, nctx, ntp, cands, kvh, group, tok),
        out_shape=jax.ShapeDtypeStruct((rows, 2 * cols), BF16),
        in_specs=[hbm] * 4 + [pl.BlockSpec(memory_space=pltpu.SMEM)] + [vmem] * 4,
        out_specs=hbm,
        scratch_shapes=[
            pltpu.VMEM((heads, tok, DH), BF16),
            pltpu.VMEM((nctx, 2 * kvh, tok, DH), BF16),
            pltpu.VMEM((cg, nctx, tok, DH), BF16),
            pltpu.VMEM((kvh, nctx, DH, tok), BF16),
            pltpu.VMEM((nctx, tok, tok), F32),
            pltpu.VMEM((2, rows, rw), BF16),
            pltpu.VMEM((nk, NC, rw, cw), BF16),
            pltpu.VMEM((nk - 1, NC, 2, rows, cw), BF16),
            pltpu.VMEM((ntp, NC, 2, rows, cw), BF16),
            pltpu.VMEM((2, NC, rows, cw), BF16),
            pltpu.VMEM((NC, rows, cw), BF16),
            dma((heads,)), dma((2 * kvh,)), dma((nk,)), dma((nk,)), dma((nctx,)),
            dma((NC,)), dma((2, nk * NC)), dma((nk * NC,)),
            dma((cands,)), dma((cands,)), dma((nk, NC)), dma((ntp, NC)),
            dma((NC,)), dma((NC,)), dma((2, NC)),
        ],
        compiler_params=pltpu.CompilerParams(
            collective_id=0, has_side_effects=True, vmem_limit_bytes=63 * 2**20),
        cost_estimate=pl.CostEstimate(
            flops=flops, bytes_accessed=4 * rw * cols * nk,
            transcendentals=nctx * tok * tok * heads * cands),
        name="attend_project",
    )(queries, keys, values, out_weight, block_keep, basec, bases, offc, offs)
    return out.reshape(cands, tok, 2 * cols)


def solution(mesh):
    return jax.shard_map(
        functools.partial(body, mesh.shape["ctx"], mesh.shape["tp"]),
        mesh=mesh,
        in_specs=(P("ctx", "tp"), P("ctx", "tp"), P("ctx", "tp"), P(), P(), P(), P("tp", "ctx")),
        out_specs=P(None, "ctx", "tp"),
        check_vma=False,
    )
```

```python
import functools
import math

import jax
import jax.numpy as jnp
from jax import lax
from jax.experimental import pallas as pl
from jax.experimental.pallas import tpu as pltpu
from jax.sharding import PartitionSpec as P

DH = 128
BLK = 128
NC = 4
THETA = 500000.0
LOW = -1e30
MESH = pl.DeviceIdType.MESH
F32 = jnp.float32
BF16 = jnp.bfloat16


def chain_kernel(nctx, ntp, cands, kvh, group, tok,
           q_hbm, k_hbm, v_hbm, w_hbm, keep_ref, basec, bases, offc, offs,
           out_hbm,
           qv, kv, krot, vt, bias, attn, wbuf, pbuf, rbuf, obuf, ybuf,
           q_sem, kv_sem, kv_up, kv_y, kv_recv, w_local, w_send, w_recv,
           a_send, a_recv, p_send, p_recv, y_send, y_recv, o_sem):
    nk = nctx // 2
    me = lax.axis_index("ctx")
    t = lax.axis_index("tp")
    k = me // 2
    y = me % 2
    other = 1 - y
    cw = wbuf.shape[3]
    rows = cands * tok
    heads = kvh * group
    has_up = k + 1 < nk
    has_down = k > 0
    mate = (me + 1 - 2 * y, t)
    up = (jnp.minimum(k + 1, nk - 1) * 2 + y, t)
    down = (jnp.maximum(k - 1, 0) * 2 + y, t)

    def remote(src, dst, ssem, rsem, dev):
        return pltpu.make_async_remote_copy(
            src_ref=src, dst_ref=dst, send_sem=ssem, recv_sem=rsem,
            device_id=dev, device_id_type=MESH)

    q_copies = [
        pltpu.make_async_copy(q_hbm.at[:, pl.ds(h * DH, DH)], qv.at[h], q_sem.at[h])
        for h in range(heads)
    ]
    kv_copies = [
        pltpu.make_async_copy(src.at[:, pl.ds(g * DH, DH)], kv.at[me, i * kvh + g],
                              kv_sem.at[i * kvh + g])
        for i, src in enumerate((k_hbm, v_hbm)) for g in range(kvh)
    ]
    w_copies = [
        pltpu.make_async_copy(w_hbm.at[:, pl.ds(n * cw, cw)], wbuf.at[k, n], w_local.at[n])
        for n in range(NC)
    ]
    for c in kv_copies + q_copies:
        c.start()

    bar = pltpu.get_barrier_semaphore()
    pl.semaphore_signal(bar, inc=1, device_id=mate, device_id_type=MESH)
    for d in range(1, ntp):
        pl.semaphore_signal(bar, inc=1, device_id=(me, lax.rem(t + d, ntp)), device_id_type=MESH)

    @pl.when(has_up)
    def _():
        pl.semaphore_signal(bar, inc=1, device_id=up, device_id_type=MESH)

    @pl.when(has_down)
    def _():
        pl.semaphore_signal(bar, inc=1, device_id=down, device_id_type=MESH)

    pl.semaphore_wait(bar, ntp + has_up.astype(jnp.int32) + has_down.astype(jnp.int32))

    def kv_up_copy(j):
        s = 2 * j + y
        return remote(kv.at[s], kv.at[s], kv_up.at[j], kv_recv.at[s], up)

    def kv_mate_copy(j, col):
        s = 2 * j + col
        return remote(kv.at[s], kv.at[s], kv_y.at[j], kv_recv.at[s], mate)

    def kv_pass(j):
        @pl.when(has_up)
        def _():
            kv_up_copy(j).start()
        kv_mate_copy(j, y).start()

    def w_up_copy(j, n, src=None):
        return remote(wbuf.at[j, n] if src is None else src, wbuf.at[j, n],
                      w_send.at[0, j * NC + n], w_recv.at[j * NC + n], up)

    def w_down_copy(j, n, src=None):
        return remote(wbuf.at[j, n] if src is None else src, wbuf.at[j, n],
                      w_send.at[1, j * NC + n], w_recv.at[j * NC + n], down)

    for c in kv_copies:
        c.wait()
    kv_pass(k)
    @pl.when(has_down)
    def _():
        for n in range(NC):
            w_down_copy(k, n, w_hbm.at[:, pl.ds(n * cw, cw)]).start()
    for c in w_copies:
        c.start()

    kio = lax.broadcasted_iota(jnp.int32, (tok, tok), 0)
    qio = lax.broadcasted_iota(jnp.int32, (tok, tok), 1)
    nb = tok // BLK

    def make_bias(j, _):
        seen = jnp.zeros((tok, tok), jnp.int32)
        for a in range(nb):
            for b in range(nb):
                here = (qio // BLK == a) & (kio // BLK == b)
                seen = jnp.where(here, keep_ref[me * nb + a, j * nb + b], seen)
        ok = (seen == 1) & (kio + (j - me) * tok <= qio)
        bias[j] = jnp.where(ok, 0.0, LOW)
        return 0

    def tables(cg, j):
        bc, bs = basec[cg], bases[cg]
        oc = offc[cg, pl.ds(j, 1)]
        os = offs[cg, pl.ds(j, 1)]
        return bc * oc - bs * os, bs * oc + bc * os

    def turn(x, c, s):
        x = x.astype(F32)
        return (x * c + pltpu.roll(x, DH // 2, 1) * s).astype(BF16)

    for s in range(1, nk):
        @pl.when(k >= s)
        def _():
            kv_up_copy(k - s).wait_recv()
            kv_pass(k - s)

    @pl.when(has_up)
    def _():
        for n in range(NC):
            w_up_copy(k, n, w_hbm.at[:, pl.ds(n * cw, cw)]).start()

    def from_mate(j, _):
        kv_mate_copy(j, other).wait_recv()
        return 0

    lax.fori_loop(0, me + 1, make_bias, 0)
    lax.fori_loop(0, k + 1, from_mate, 0)

    def prepare(j, _):
        for g in range(kvh):
            vt[g, j] = jnp.transpose(kv[j, kvh + g].astype(F32)).astype(BF16)
            x = kv[j, g]
            for c in range(cands):
                cc, ss = tables(c * kvh + g, j)
                krot[c * kvh + g, j] = turn(x, cc, ss)
        return 0

    lax.fori_loop(0, me + 1, prepare, 0)
    for c in q_copies:
        c.wait()

    def forward(s, n):
        @pl.when((k >= s) & has_up)
        def _():
            w_up_copy(k - s, n).wait_recv()
            w_up_copy(k - s, n).start()

        @pl.when((k + s < nk) & has_down)
        def _():
            w_down_copy(k + s, n).wait_recv()
            w_down_copy(k + s, n).start()

    wide = 4
    per_c = kvh * group // wide
    c2 = DH ** (-0.5) * math.log2(math.e)

    def attn_copy(c, col):
        part = attn.at[col, pl.ds(c * tok, tok)]
        return remote(part, part, a_send.at[c], a_recv.at[c], mate)

    def candidate(c, _):
        def unit(i, _):
            g = i // (group // wide)
            cg = c * kvh + g
            h0 = wide * i
            cc, ss = tables(cg, me)
            qr = [turn(qv[h0 + d], cc, ss) for d in range(wide)]

            def step(j, state):
                kt = krot[cg, j]
                vv = vt[g, j]
                bj = bias[j]
                new = []
                sts = [lax.dot_general(kt, qr[d], (((1,), (1,)), ((), ())),
                                       preferred_element_type=F32) + bj
                       for d in range(wide)]
                for d in range(wide):
                    m, l, acc = state[d]
                    st = sts[d]
                    mn = jnp.maximum(m, jnp.max(st, axis=0, keepdims=True))
                    p = jnp.exp2((st - mn) * c2)
                    al = jnp.exp2((m - mn) * c2)
                    l = l * al + jnp.sum(p, axis=0, keepdims=True)
                    acc = acc * al + jnp.dot(vv, p.astype(BF16), preferred_element_type=F32)
                    new.append((mn, l, acc))
                return tuple(new)

            one = (jnp.full((1, tok), LOW, F32), jnp.zeros((1, tok), F32),
                   jnp.zeros((DH, tok), F32))
            state = lax.fori_loop(0, me + 1, step, (one,) * wide)
            for d in range(wide):
                m, l, acc = state[d]
                at = pl.multiple_of((h0 + d) * DH, DH)
                attn[y, pl.ds(pl.multiple_of(c * tok, tok), tok), pl.ds(at, DH)] = (
                    jnp.transpose(acc / l).astype(BF16))
            return 0

        lax.fori_loop(0, per_c, unit, 0)
        attn_copy(c, y).start()
        return 0

    lax.fori_loop(0, cands, candidate, 0)
    for c in w_copies:
        c.wait()
    for c in range(cands):
        attn_copy(c, other).wait_recv()

    def slot(j):
        return jnp.minimum(j - (j > t).astype(jnp.int32), nk - 2)

    def p_copy(j, n):
        return remote(pbuf.at[slot(j), n], rbuf.at[t, n], p_send.at[j, n], p_recv.at[t, n], (me, j))

    def p_arrive(src, n):
        return remote(rbuf.at[src, n], rbuf.at[src, n], p_send.at[src, n], p_recv.at[src, n],
                      (me, src))

    def y_copy(n, col):
        return remote(ybuf.at[n], obuf.at[col, n], y_send.at[n], y_recv.at[n], mate)

    def o_copy(col, n):
        return pltpu.make_async_copy(
            obuf.at[col, n],
            out_hbm.at[:, pl.ds(pl.multiple_of((col * NC + n) * cw, cw), cw)],
            o_sem.at[col, n])

    def project(j, n, dest):
        def block(half, _):
            dest[half] = jnp.dot(
                attn[half], wbuf[j, n], preferred_element_type=F32).astype(BF16)
            return 0
        lax.fori_loop(0, 2, block, 0)

    def compute(p, d, n):
        j = k - p if d == 0 else k + p
        ok = k >= p if d == 0 else k + p < nk
        fwd = has_up if d == 0 else has_down
        if p > 0:
            @pl.when(ok & jnp.logical_not(fwd))
            def _():
                (w_up_copy if d == 0 else w_down_copy)(j, n).wait_recv()
        @pl.when(ok & (j != t))
        def _():
            project(j, n, pbuf.at[slot(j), n])
            p_copy(j, n).start()

        @pl.when(ok & (j == t))
        def _():
            project(j, n, rbuf.at[t, n])

    def finish(n):
        for d in range(1, ntp):
            p_arrive(lax.rem(t + d, ntp), n).wait_recv()

        def total(half, r):
            acc = rbuf[0, n, half, pl.ds(r, BLK)].astype(F32)
            for src in range(1, ntp):
                acc = acc + rbuf[src, n, half, pl.ds(r, BLK)].astype(F32)
            return acc.astype(BF16)

        def block(b, _):
            r = pl.multiple_of(b * BLK, BLK)
            ybuf[n, pl.ds(r, BLK)] = total(other, r)
            return 0

        lax.fori_loop(0, rows // BLK, block, 0)
        y_copy(n, y).start()

        def block2(b, _):
            r = pl.multiple_of(b * BLK, BLK)
            obuf[y, n, pl.ds(r, BLK)] = total(y, r)
            return 0

        lax.fori_loop(0, rows // BLK, block2, 0)
        o_copy(y, n).start()

    for p in range(nk):
        mine = (t == k - p) | (t == k + p)

        if 0 < p < nk - 1:
            def pass_on(n, _):
                forward(p, n)
                return 0
            lax.fori_loop(0, NC, pass_on, 0)

        def chunk(n, _):
            compute(p, 0, n)
            if p > 0:
                compute(p, 1, n)

            @pl.when(mine & (n > 0))
            def _():
                finish(n - 1)
            return 0

        lax.fori_loop(0, NC, chunk, 0)

        @pl.when(mine)
        def _():
            finish(NC - 1)

    def drain(n, _):
        y_copy(n, other).wait_recv()
        o_copy(other, n).start()
        return 0

    lax.fori_loop(0, NC, drain, 0)

    def drain2(n, _):
        def sent(j, _):
            @pl.when(j != t)
            def _():
                p_copy(j, n).wait_send()
            return 0
        lax.fori_loop(0, nk, sent, 0)
        y_copy(n, y).wait_send()
        o_copy(y, n).wait()
        o_copy(other, n).wait()
        return 0

    lax.fori_loop(0, NC, drain2, 0)
    for c in range(cands):
        attn_copy(c, y).wait_send()

    def drain_kv(j, _):
        @pl.when(has_up)
        def _():
            kv_up_copy(j).wait_send()

            def each(n, _):
                w_up_copy(j, n).wait_send()
                return 0
            lax.fori_loop(0, NC, each, 0)
        kv_mate_copy(j, y).wait_send()
        return 0

    lax.fori_loop(0, k + 1, drain_kv, 0)

    @pl.when(has_down)
    def _():
        def drain_down(j, _):
            def each(n, _):
                w_down_copy(j, n).wait_send()
                return 0
            lax.fori_loop(0, NC, each, 0)
            return 0
        lax.fori_loop(k, nk, drain_down, 0)


ISSUE = (
    (0, 0, 0, 0),
    (1, 1, 1, 1),
    (0, 0, 0, 0),
    (0, 0, 0, 0),
)
LAG = 8
ORDER = (
    ((0, 0, 0, 0), (0, 1, 0, 0), (0, 2, 0, 0), (0, 3, 0, 0), (0, 0, 1, 0), (0, 1, 1, 0), (0, 2, 1, 0), (0, 3, 1, 0), (0, 0, 2, 0), (0, 1, 2, 0), (0, 2, 2, 0), (0, 3, 2, 0)),
    ((1, 0, 0, 0), (0, 0, 0, 1), (1, 0, 1, 0), (0, 1, 0, 1), (1, 0, 2, 0), (0, 2, 0, 1), (1, 0, 0, 1), (0, 3, 0, 1)),
    ((1, 1, 0, 0), (1, 1, 1, 0), (1, 1, 2, 0), (1, 1, 0, 1)),
    ((1, 0, 1, 1), (0, 0, 1, 1), (1, 1, 1, 1), (0, 1, 1, 1), (0, 2, 1, 1), (0, 3, 1, 1)),
    ((1, 2, 0, 0), (1, 2, 1, 0), (1, 2, 2, 0), (1, 2, 0, 1), (1, 2, 1, 1)),
    ((0, 0, 2, 1), (1, 0, 2, 1), (0, 1, 2, 1), (1, 1, 2, 1), (0, 2, 2, 1), (1, 2, 2, 1), (0, 3, 2, 1)),
    ((1, 3, 0, 0), (1, 3, 1, 0), (1, 3, 2, 0), (1, 3, 0, 1), (1, 3, 1, 1), (1, 3, 2, 1)),
)
NEEDS = ((), ((0,), (0,), False), ((), (1,), False), ((1,), (), True),
         ((), (2,), True), ((2,), (), False), ((), (3,), True))


def quad_fits(nctx, ntp, cands, cols):
    return nctx == 8 and ntp == 4 and cands == 3 and cols % (NC * DH) == 0


def quad_kernel(cands, kvh, group, tok,
                q_hbm, k_hbm, v_hbm, w_hbm, keep_ref, basec, bases, offc, offs,
                out_hbm,
                qv, kv, krot, vt, bias, attn, wbuf, give, kept, got, xgot,
                q_sem, kv_sem, kv_up, kv_y, kv_near, kv_recv, w_local, w_send, w_recv,
                a_send, a_recv, g_send, g_recv, x_send, x_recv, o_send, o_recv):
    nz = 4
    me = lax.axis_index("ctx")
    t = lax.axis_index("tp")
    z, y = me // 2, me % 2
    zh, zl = z // 2, z % 2
    x, core = t // 2, t % 2
    cw = wbuf.shape[3]
    heads = kvh * group
    half = 2 * tok
    width = group * DH
    has_up = z + 1 < nz
    has_down = z > 0
    one = jnp.int32(1)

    mate = (z * 2 + 1 - y, t)
    up = (jnp.minimum(z + 1, nz - 1) * 2 + y, t)
    down = (jnp.maximum(z - 1, 0) * 2 + y, t)
    near = ((zh * 2 + 1 - zl) * 2 + y, t)
    far = (((1 - zh) * 2 + zl) * 2 + y, t)
    sibling = (me, x * 2 + 1 - core)
    across = (me, (1 - x) * 2 + core)
    at_home = (zl == core) & (core == y)

    def remote(src, dst, ssem, rsem, dev):
        return pltpu.make_async_remote_copy(
            src_ref=src, dst_ref=dst, send_sem=ssem, recv_sem=rsem,
            device_id=dev, device_id_type=MESH)

    q_local = pltpu.make_async_copy(q_hbm, qv.at[zl], q_sem.at[0])
    q_near = remote(q_hbm, qv.at[zl], q_sem.at[1], q_sem.at[2], near)
    q_from = remote(q_hbm, qv.at[1 - zl], q_sem.at[1], q_sem.at[2], near)
    kv_copies = [
        pltpu.make_async_copy(src.at[:, pl.ds(g * DH, DH)], kv.at[me, i * kvh + g],
                              kv_sem.at[i * kvh + g])
        for i, src in enumerate((k_hbm, v_hbm)) for g in range(kvh)
    ]
    w_copies = [
        pltpu.make_async_copy(w_hbm.at[:, pl.ds(n * cw, cw)], wbuf.at[0, n], w_local.at[n])
        for n in range(NC)
    ]
    for c in kv_copies + [q_local]:
        c.start()

    def out_target(zt):
        return ((zh * 2 + zt) * 2 + core, x * 2 + zl)

    def out_source(col):
        return ((zh * 2 + core) * 2 + col, x * 2 + y)

    bar = pltpu.get_barrier_semaphore()
    for dev in (mate, near, far, sibling, across):
        pl.semaphore_signal(bar, inc=1, device_id=dev, device_id_type=MESH)

    @pl.when(has_down)
    def _():
        pl.semaphore_signal(bar, inc=1, device_id=down, device_id_type=MESH)

    for col in range(2):
        @pl.when(jnp.logical_not(at_home & (col == y)))
        def _():
            pl.semaphore_signal(bar, inc=1, device_id=out_source(col), device_id_type=MESH)

    pl.semaphore_wait(bar, 7 + has_up.astype(jnp.int32) - at_home.astype(jnp.int32))

    def kv_up_copy(j):
        s = 2 * j + y
        return remote(kv.at[s], kv.at[s], kv_up.at[j], kv_recv.at[s], up)

    def kv_mate_copy(j, col):
        s = 2 * j + col
        return remote(kv.at[s], kv.at[s], kv_y.at[j], kv_recv.at[s], mate)

    def kv_pass(j):
        @pl.when(has_up)
        def _():
            kv_up_copy(j).start()
        kv_mate_copy(j, y).start()

    def kv_near_copy(zz):
        s = 2 * zz + y
        return remote(kv.at[s], kv.at[s], kv_near.at[0], kv_recv.at[s], near)

    def w_copy(n):
        return remote(w_hbm.at[:, pl.ds(n * cw, cw)], wbuf.at[1, n],
                      w_send.at[n], w_recv.at[n], far)

    def issue(point):
        for zz in range(nz):
            for n in range(NC):
                if ISSUE[zz][n] in (point if isinstance(point, range) else (point,)):
                    here = z == zz

                    @pl.when(here)
                    def _():
                        w_copy(n).start()

    for c in kv_copies:
        c.wait()
    kv_pass(z)

    @pl.when(zl == 1)
    def _():
        kv_near_copy(z).start()
        q_near.start()

    @pl.when(z == 0)
    def _():
        q_near.start()

    issue(0)
    for c in w_copies:
        c.start()

    top = (zh * 2 + 1) * 2 + y
    blocks = bias.shape[1]
    kio = lax.broadcasted_iota(jnp.int32, (tok, tok), 0)
    qio = lax.broadcasted_iota(jnp.int32, (tok, tok), 1)
    nb = tok // BLK

    def make_bias(i, _):
        zt, j = i // blocks, i % blocks
        mine = (zh * 2 + zt) * 2 + y
        seen = jnp.zeros((tok, tok), jnp.int32)
        for a in range(nb):
            for b in range(nb):
                here = (qio // BLK == a) & (kio // BLK == b)
                seen = jnp.where(here, keep_ref[mine * nb + a, j * nb + b], seen)
        ok = (seen == 1) & (kio + (j - mine) * tok <= qio)
        bias[zt, j] = jnp.where(ok, 0.0, LOW)
        return 0

    def tables(cg, j):
        bc, bs = basec[cg], bases[cg]
        oc = offc[cg, pl.ds(j, 1)]
        os = offs[cg, pl.ds(j, 1)]
        return bc * oc - bs * os, bs * oc + bc * os

    def turn(v, c, s):
        v = v.astype(F32)
        return (v * c + pltpu.roll(v, DH // 2, 1) * s).astype(BF16)

    def prepare(zz):
        kv_mate_copy(zz, 1 - y).wait_recv()

        def block(j, _):
            for g in range(kvh):
                vt[g, j] = jnp.transpose(kv[j, kvh + g].astype(F32)).astype(BF16)
                v = kv[j, g]
                for c in range(cands):
                    cc, ss = tables(c * kvh + g, j)
                    krot[c * kvh + g, j] = turn(v, cc, ss)
            return 0

        lax.fori_loop(2 * zz, 2 * zz + 2, block, 0)

    lax.fori_loop(0, 2 * blocks, make_bias, 0)

    def fetch(s, _):
        kv_up_copy(z - s).wait_recv()
        kv_pass(z - s)
        prepare(z - s + 1)
        return 0

    lax.fori_loop(1, z + 1, fetch, 0)

    @pl.when(zl == 0)
    def _():
        @pl.when(z > 0)
        def _():
            q_near.start()
        kv_near_copy(z + 1).wait_recv()
        kv_mate_copy(z + 1, y).start()

    issue(1)
    prepare(jnp.int32(0))

    @pl.when(zl == 0)
    def _():
        prepare(z + 1)

    q_local.wait()
    q_from.wait_recv()

    pieces = cands * kvh
    c2 = DH ** (-0.5) * math.log2(math.e)

    def a_copy(i, ty, zt):
        c, g = i // kvh, i % kvh
        p = attn.at[c, pl.ds(pl.multiple_of((ty * 2 + zt) * tok, tok), tok),
                    pl.ds(pl.multiple_of(g * width, width), width)]
        return remote(p, p, a_send.at[zt, i], a_recv.at[zt, i], mate)

    def attend(i, zt):
        c, g = i // kvh, i % kvh
        mine = (zh * 2 + zt) * 2 + y
        cc, ss = tables(i, mine)
        qr = [turn(qv[zt, :, pl.ds(pl.multiple_of((g * group + d) * DH, DH), DH)], cc, ss)
              for d in range(group)]

        def step(j, state):
            js = [2 * j, jnp.minimum(2 * j + 1, top)]
            bs = [bias[zt, 2 * j], bias[zt, 2 * j + 1]]
            new = []
            sts = [[lax.dot_general(krot[i, jj], qr[d], (((1,), (1,)), ((), ())),
                                    preferred_element_type=F32) + bj
                    for jj, bj in zip(js, bs)] for d in range(group)]
            for d in range(group):
                m, l, acc = state[d]
                mn = m
                for st in sts[d]:
                    mn = jnp.maximum(mn, jnp.max(st, axis=0, keepdims=True))
                al = jnp.exp2((m - mn) * c2)
                l, acc = l * al, acc * al
                for jj, st in zip(js, sts[d]):
                    p = jnp.exp2((st - mn) * c2)
                    l = l + jnp.sum(p, axis=0, keepdims=True)
                    acc = acc + jnp.dot(vt[g, jj], p.astype(BF16), preferred_element_type=F32)
                new.append((mn, l, acc))
            return tuple(new)

        first = (jnp.full((1, tok), LOW, F32), jnp.zeros((1, tok), F32),
                 jnp.zeros((DH, tok), F32))
        state = lax.fori_loop(0, mine // 2 + 1, step, (first,) * group)
        for d in range(group):
            m, l, acc = state[d]
            at = pl.multiple_of((g * group + d) * DH, DH)
            attn[c, pl.ds(pl.multiple_of((y * 2 + zt) * tok, tok), tok), pl.ds(at, DH)] = (
                jnp.transpose(acc / l).astype(BF16))

    def piece(i, _):
        def both(k, _):
            zt = zl + k * (1 - 2 * zl)
            attend(i, zt)
            a_copy(i, y, zt).start()
            return 0

        lax.fori_loop(0, 2, both, 0)
        for zz in range(nz):
            for n in range(NC):
                if 2 <= ISSUE[zz][n] < 2 + pieces:
                    @pl.when((z == zz) & (i == ISSUE[zz][n] - 2))
                    def _():
                        w_copy(n).start()
        return 0


    def need_attn(c):
        for g in range(kvh):
            for zt in range(2):
                a_copy(c * kvh + g, 1 - y, zt).wait_recv()

    table = [v for seg in ORDER for v in seg]

    def unit_of(u):
        block = u // 12
        sh = 2 * (u % 12)

        def pick(k):
            word = jnp.int32(0)
            for b in range(0, len(table), 12):
                bits = sum(v[k] << (2 * i) for i, v in enumerate(table[b:b + 12]))
                word = jnp.where(block == b // 12, jnp.int32(bits), word)
            return lax.shift_right_logical(word, sh) & 3

        return pick(0), pick(1), pick(2), pick(3)

    def receives(w):
        return jnp.where(w == 0, zh, 1 - zh) == x

    def g_copy(u):
        return remote(give.at[u], got.at[u], g_send.at[u], g_recv.at[u], sibling)

    def x_copy(u, n, c):
        i = n * cands + c
        return remote(kept.at[u], xgot.at[i], x_send.at[i], x_recv.at[i], across)

    def o_ref(n, c, col):
        return out_hbm.at[pl.ds(pl.multiple_of(c * tok, tok), tok),
                          pl.ds(pl.multiple_of((col * NC + n) * cw, cw), cw)]

    def o_copy(u, n, c, zt):
        return remote(kept.at[u, pl.ds(zt * tok, tok)], o_ref(n, c, y),
                      o_send.at[zt, n * cands + c], o_recv.at[y, n * cands + c], out_target(zt))

    def o_local(u, n, c, zt):
        return pltpu.make_async_copy(kept.at[u, pl.ds(zt * tok, tok)], o_ref(n, c, y),
                                     o_send.at[zt, n * cands + c])

    def slot(w, n, c):
        return (w * NC + n) * cands + c

    def reduces(h):
        return (h == 0) == (core == y)

    def multiply(u):
        w, n, c, h = unit_of(u)
        i = slot(w, n, c)
        r = pl.multiple_of(jnp.where(h == 0, y, 1 - y) * half, half)
        p = jnp.dot(attn[c, pl.ds(r, half)], wbuf[w, n], preferred_element_type=F32).astype(BF16)

        @pl.when(reduces(h))
        def _():
            kept[i] = p

        @pl.when(jnp.logical_not(reduces(h)))
        def _():
            give[i] = p
            g_copy(i).start()

    def pair(u):
        w, n, c, h = unit_of(u)
        i = slot(w, n, c)

        @pl.when(reduces(h) & jnp.logical_not(receives(w)))
        def _():
            g_copy(i).wait_recv()

            def block(b, _):
                r = pl.ds(pl.multiple_of(b * BLK, BLK), BLK)
                kept[i, r] = (kept[i, r].astype(F32) + got[i, r].astype(F32)).astype(BF16)
                return 0

            lax.fori_loop(0, half // BLK, block, 0)
            x_copy(i, n, c).start()

    def finish(u):
        w, n, c, h = unit_of(u)
        i = slot(w, n, c)

        @pl.when(reduces(h) & receives(w))
        def _():
            g_copy(i).wait_recv()
            x_copy(i, n, c).wait_recv()

            def block(b, _):
                r = pl.ds(pl.multiple_of(b * BLK, BLK), BLK)
                kept[i, r] = (kept[i, r].astype(F32) + got[i, r].astype(F32)
                              + xgot[n * cands + c, r].astype(F32)).astype(BF16)
                return 0

            lax.fori_loop(0, half // BLK, block, 0)
            for zt in range(2):
                own = at_home & (zl == zt)

                @pl.when(own)
                def _():
                    o_local(i, n, c, zt).start()

                @pl.when(jnp.logical_not(own))
                def _():
                    o_copy(i, n, c, zt).start()

    for c in w_copies:
        c.wait()

    def candidate(c, _):
        lax.fori_loop(c * kvh, (c + 1) * kvh, piece, 0)

        def own(u, _):
            multiply(u)

            @pl.when(u > NC * c)
            def _():
                pair(u - 1)
            return 0

        def old(u, _):
            finish(u)
            return 0

        lax.fori_loop(NC * c, NC * (c + 1), own, 0)
        pair(NC * (c + 1) - 1)
        lax.fori_loop(NC * jnp.maximum(c - 1, 0), NC * c, old, 0)
        return 0

    lax.fori_loop(0, cands, candidate, 0)
    issue(2 + pieces)
    done = NC * (cands - 1)

    def stretch(lo, hi, lag, flush):
        nonlocal done

        def step(u, _):
            multiply(u)

            @pl.when(u > lo)
            def _():
                pair(u - 1)

            @pl.when(u - lag >= done)
            def _():
                finish(u - lag)
            return 0

        def rest(u, _):
            finish(u)
            return 0

        lax.fori_loop(lo, hi, step, 0)
        pair(jnp.int32(hi - 1))
        done = max(done, hi - lag)
        if flush:
            lax.fori_loop(done, hi, rest, 0)
            done = hi

    def need_w(n):
        w_copy(n).wait_recv()

    marks = [0]
    for seg in ORDER:
        marks.append(marks[-1] + len(seg))
    for seg, (attn_of, w_of, flush) in enumerate(NEEDS[1:], 1):
        for c in attn_of:
            need_attn(c)
        for n in w_of:
            need_w(n)
        stretch(marks[seg], marks[seg + 1], LAG, flush)
        issue(3 + pieces + seg)

    def arrived(i, _):
        n, c = i // cands, i % cands
        for col in range(2):
            @pl.when(jnp.logical_not(at_home & (col == y)))
            def _():
                remote(o_ref(n, c, col), o_ref(n, c, col), o_send.at[0, i], o_recv.at[col, i],
                       out_source(col)).wait_recv()
        return 0

    lax.fori_loop(0, NC * cands, arrived, 0)

    def drain(u, _):
        w, n, c = u // (NC * cands), (u // cands) % NC, u % cands
        g_copy(u).wait_send()

        @pl.when(receives(w))
        def _():
            for zt in range(2):
                own = at_home & (zl == zt)

                @pl.when(own)
                def _():
                    o_local(u, n, c, zt).wait()

                @pl.when(jnp.logical_not(own))
                def _():
                    o_copy(u, n, c, zt).wait_send()

        @pl.when(jnp.logical_not(receives(w)))
        def _():
            x_copy(u, n, c).wait_send()
        return 0

    lax.fori_loop(0, 2 * NC * cands, drain, 0)

    def drain_attn(i, _):
        for zt in range(2):
            a_copy(i, y, zt).wait_send()
        return 0

    lax.fori_loop(0, pieces, drain_attn, 0)
    for n in range(NC):
        w_copy(n).wait_send()

    q_near.wait_send()

    @pl.when(zl == 1)
    def _():
        kv_near_copy(z).wait_send()

    @pl.when(zl == 0)
    def _():
        kv_mate_copy(z + 1, y).wait_send()

    def drain_kv(j, _):
        @pl.when(has_up)
        def _():
            kv_up_copy(j).wait_send()
        kv_mate_copy(j, y).wait_send()
        return 0

    lax.fori_loop(0, z + 1, drain_kv, 0)


def quad(nctx, ntp, cands, kvh, group, tok, rw, cols,
         queries, keys, values, out_weight, block_keep, basec, bases, offc, offs):
    heads = kvh * group
    cg = cands * kvh
    cw = cols // NC
    units = 2 * NC * cands
    hbm = pl.BlockSpec(memory_space=pl.ANY)
    vmem = pl.BlockSpec(memory_space=pltpu.VMEM)
    dma = pltpu.SemaphoreType.DMA
    return pl.pallas_call(
        functools.partial(quad_kernel, cands, kvh, group, tok),
        out_shape=jax.ShapeDtypeStruct((cands * tok, 2 * cols), BF16),
        in_specs=[hbm] * 4 + [pl.BlockSpec(memory_space=pltpu.SMEM)] + [vmem] * 4,
        out_specs=hbm,
        scratch_shapes=[
            pltpu.VMEM((2, tok, heads * DH), BF16),
            pltpu.VMEM((nctx, 2 * kvh, tok, DH), BF16),
            pltpu.VMEM((cg, nctx, tok, DH), BF16),
            pltpu.VMEM((kvh, nctx, DH, tok), BF16),
            pltpu.VMEM((2, nctx, tok, tok), F32),
            pltpu.VMEM((cands, 4 * tok, rw), BF16),
            pltpu.VMEM((2, NC, rw, cw), BF16),
            pltpu.VMEM((units, 2 * tok, cw), BF16),
            pltpu.VMEM((units, 2 * tok, cw), BF16),
            pltpu.VMEM((units, 2 * tok, cw), BF16),
            pltpu.VMEM((NC * cands, 2 * tok, cw), BF16),
            dma((3,)), dma((2 * kvh,)), dma((nctx // 2,)), dma((nctx // 2,)), dma((1,)), dma((nctx,)),
            dma((NC,)), dma((NC,)), dma((NC,)),
            dma((2, cg)), dma((2, cg)), dma((units,)), dma((units,)),
            dma((NC * cands,)), dma((NC * cands,)), dma((2, NC * cands)), dma((2, NC * cands)),
        ],
        compiler_params=pltpu.CompilerParams(
            collective_id=0, has_side_effects=True, vmem_limit_bytes=63 * 2**20),
        cost_estimate=pl.CostEstimate(
            flops=4 * nctx * tok * tok * heads * cands * DH + 4 * 4 * cands * tok * rw * cols,
            bytes_accessed=4 * rw * cols * 2,
            transcendentals=nctx * tok * tok * heads * cands),
        name="attend_project",
    )(queries, keys, values, out_weight, block_keep, basec, bases, offc, offs)


def body(nctx, ntp, queries, keys, values, block_keep, scale_pick, scale_table, out_weight):
    tok = queries.shape[0]
    kvh = keys.shape[1] // DH
    group = queries.shape[1] // (kvh * DH)
    cands = scale_pick.shape[0]
    kv_all = scale_pick.shape[1]
    table_rows = scale_table.shape[0]
    rw, cols = out_weight.shape
    nk = nctx // 2
    cw = cols // NC
    heads = kvh * group
    rows = cands * tok
    here = lax.axis_index("tp") * kvh + jnp.arange(kvh, dtype=jnp.int32)
    select = jnp.arange(kv_all, dtype=jnp.int32)[None, :] == here[:, None]
    picks = jnp.sum(jnp.where(select[None], scale_pick[:, None, :], 0), axis=-1)
    hit = picks[..., None] == jnp.arange(table_rows, dtype=jnp.int32)
    scales = jnp.sum(jnp.where(hit[..., None], scale_table[None, None], 0.0), axis=2)
    inv = 1.0 / THETA ** (jnp.arange(DH // 2, dtype=F32) * 2.0 / DH)
    freq = (inv / scales).reshape(cands * kvh, 1, DH // 2)

    def table(positions):
        angle = positions.astype(F32)[None, :, None] * freq
        c, s = jnp.cos(angle), jnp.sin(angle)
        return jnp.concatenate([c, c], -1), jnp.concatenate([-s, s], -1)

    basec, bases = table(jnp.arange(tok, dtype=jnp.int32))
    offc, offs = table(jnp.arange(nctx, dtype=jnp.int32) * tok)
    cg = cands * kvh
    hbm = pl.BlockSpec(memory_space=pl.ANY)
    vmem = pl.BlockSpec(memory_space=pltpu.VMEM)
    dma = pltpu.SemaphoreType.DMA
    if quad_fits(nctx, ntp, cands, cols):
        out = quad(nctx, ntp, cands, kvh, group, tok, rw, cols,
                   queries, keys, values, out_weight, block_keep, basec, bases, offc, offs)
        return out.reshape(cands, tok, 2 * cols)
    flops = 4 * nctx * tok * tok * heads * cands * DH + 4 * rows * rw * cols * nk
    out = pl.pallas_call(
        functools.partial(chain_kernel, nctx, ntp, cands, kvh, group, tok),
        out_shape=jax.ShapeDtypeStruct((rows, 2 * cols), BF16),
        in_specs=[hbm] * 4 + [pl.BlockSpec(memory_space=pltpu.SMEM)] + [vmem] * 4,
        out_specs=hbm,
        scratch_shapes=[
            pltpu.VMEM((heads, tok, DH), BF16),
            pltpu.VMEM((nctx, 2 * kvh, tok, DH), BF16),
            pltpu.VMEM((cg, nctx, tok, DH), BF16),
            pltpu.VMEM((kvh, nctx, DH, tok), BF16),
            pltpu.VMEM((nctx, tok, tok), F32),
            pltpu.VMEM((2, rows, rw), BF16),
            pltpu.VMEM((nk, NC, rw, cw), BF16),
            pltpu.VMEM((nk - 1, NC, 2, rows, cw), BF16),
            pltpu.VMEM((ntp, NC, 2, rows, cw), BF16),
            pltpu.VMEM((2, NC, rows, cw), BF16),
            pltpu.VMEM((NC, rows, cw), BF16),
            dma((heads,)), dma((2 * kvh,)), dma((nk,)), dma((nk,)), dma((nctx,)),
            dma((NC,)), dma((2, nk * NC)), dma((nk * NC,)),
            dma((cands,)), dma((cands,)), dma((nk, NC)), dma((ntp, NC)),
            dma((NC,)), dma((NC,)), dma((2, NC)),
        ],
        compiler_params=pltpu.CompilerParams(
            collective_id=0, has_side_effects=True, vmem_limit_bytes=63 * 2**20),
        cost_estimate=pl.CostEstimate(
            flops=flops, bytes_accessed=4 * rw * cols * nk,
            transcendentals=nctx * tok * tok * heads * cands),
        name="attend_project",
    )(queries, keys, values, out_weight, block_keep, basec, bases, offc, offs)
    return out.reshape(cands, tok, 2 * cols)


def solution(mesh):
    return jax.shard_map(
        functools.partial(body, mesh.shape["ctx"], mesh.shape["tp"]),
        mesh=mesh,
        in_specs=(P("ctx", "tp"), P("ctx", "tp"), P("ctx", "tp"), P(), P(), P(), P("tp", "ctx")),
        out_specs=P(None, "ctx", "tp"),
        check_vma=False,
    )
```

```python
import functools
import math

import jax
import jax.numpy as jnp
from jax import lax
from jax.experimental import pallas as pl
from jax.experimental.pallas import tpu as pltpu
from jax.sharding import PartitionSpec as P

DH = 128
BLK = 128
NC = 4
THETA = 500000.0
LOW = -1e30
MESH = pl.DeviceIdType.MESH
F32 = jnp.float32
BF16 = jnp.bfloat16


def chain_kernel(nctx, ntp, cands, kvh, group, tok,
           q_hbm, k_hbm, v_hbm, w_hbm, keep_ref, basec, bases, offc, offs,
           out_hbm,
           qv, kv, krot, vt, bias, attn, wbuf, pbuf, rbuf, obuf, ybuf,
           q_sem, kv_sem, kv_up, kv_y, kv_recv, w_local, w_send, w_recv,
           a_send, a_recv, p_send, p_recv, y_send, y_recv, o_sem):
    nk = nctx // 2
    me = lax.axis_index("ctx")
    t = lax.axis_index("tp")
    k = me // 2
    y = me % 2
    other = 1 - y
    cw = wbuf.shape[3]
    rows = cands * tok
    heads = kvh * group
    has_up = k + 1 < nk
    has_down = k > 0
    mate = (me + 1 - 2 * y, t)
    up = (jnp.minimum(k + 1, nk - 1) * 2 + y, t)
    down = (jnp.maximum(k - 1, 0) * 2 + y, t)

    def remote(src, dst, ssem, rsem, dev):
        return pltpu.make_async_remote_copy(
            src_ref=src, dst_ref=dst, send_sem=ssem, recv_sem=rsem,
            device_id=dev, device_id_type=MESH)

    q_copies = [
        pltpu.make_async_copy(q_hbm.at[:, pl.ds(h * DH, DH)], qv.at[h], q_sem.at[h])
        for h in range(heads)
    ]
    kv_copies = [
        pltpu.make_async_copy(src.at[:, pl.ds(g * DH, DH)], kv.at[me, i * kvh + g],
                              kv_sem.at[i * kvh + g])
        for i, src in enumerate((k_hbm, v_hbm)) for g in range(kvh)
    ]
    w_copies = [
        pltpu.make_async_copy(w_hbm.at[:, pl.ds(n * cw, cw)], wbuf.at[k, n], w_local.at[n])
        for n in range(NC)
    ]
    for c in kv_copies + q_copies:
        c.start()

    bar = pltpu.get_barrier_semaphore()
    pl.semaphore_signal(bar, inc=1, device_id=mate, device_id_type=MESH)
    for d in range(1, ntp):
        pl.semaphore_signal(bar, inc=1, device_id=(me, lax.rem(t + d, ntp)), device_id_type=MESH)

    @pl.when(has_up)
    def _():
        pl.semaphore_signal(bar, inc=1, device_id=up, device_id_type=MESH)

    @pl.when(has_down)
    def _():
        pl.semaphore_signal(bar, inc=1, device_id=down, device_id_type=MESH)

    pl.semaphore_wait(bar, ntp + has_up.astype(jnp.int32) + has_down.astype(jnp.int32))

    def kv_up_copy(j):
        s = 2 * j + y
        return remote(kv.at[s], kv.at[s], kv_up.at[j], kv_recv.at[s], up)

    def kv_mate_copy(j, col):
        s = 2 * j + col
        return remote(kv.at[s], kv.at[s], kv_y.at[j], kv_recv.at[s], mate)

    def kv_pass(j):
        @pl.when(has_up)
        def _():
            kv_up_copy(j).start()
        kv_mate_copy(j, y).start()

    def w_up_copy(j, n, src=None):
        return remote(wbuf.at[j, n] if src is None else src, wbuf.at[j, n],
                      w_send.at[0, j * NC + n], w_recv.at[j * NC + n], up)

    def w_down_copy(j, n, src=None):
        return remote(wbuf.at[j, n] if src is None else src, wbuf.at[j, n],
                      w_send.at[1, j * NC + n], w_recv.at[j * NC + n], down)

    for c in kv_copies:
        c.wait()
    kv_pass(k)
    @pl.when(has_down)
    def _():
        for n in range(NC):
            w_down_copy(k, n, w_hbm.at[:, pl.ds(n * cw, cw)]).start()
    for c in w_copies:
        c.start()

    kio = lax.broadcasted_iota(jnp.int32, (tok, tok), 0)
    qio = lax.broadcasted_iota(jnp.int32, (tok, tok), 1)
    nb = tok // BLK

    def make_bias(j, _):
        seen = jnp.zeros((tok, tok), jnp.int32)
        for a in range(nb):
            for b in range(nb):
                here = (qio // BLK == a) & (kio // BLK == b)
                seen = jnp.where(here, keep_ref[me * nb + a, j * nb + b], seen)
        ok = (seen == 1) & (kio + (j - me) * tok <= qio)
        bias[j] = jnp.where(ok, 0.0, LOW)
        return 0

    def tables(cg, j):
        bc, bs = basec[cg], bases[cg]
        oc = offc[cg, pl.ds(j, 1)]
        os = offs[cg, pl.ds(j, 1)]
        return bc * oc - bs * os, bs * oc + bc * os

    def turn(x, c, s):
        x = x.astype(F32)
        return (x * c + pltpu.roll(x, DH // 2, 1) * s).astype(BF16)

    for s in range(1, nk):
        @pl.when(k >= s)
        def _():
            kv_up_copy(k - s).wait_recv()
            kv_pass(k - s)

    @pl.when(has_up)
    def _():
        for n in range(NC):
            w_up_copy(k, n, w_hbm.at[:, pl.ds(n * cw, cw)]).start()

    def from_mate(j, _):
        kv_mate_copy(j, other).wait_recv()
        return 0

    lax.fori_loop(0, me + 1, make_bias, 0)
    lax.fori_loop(0, k + 1, from_mate, 0)

    def prepare(j, _):
        for g in range(kvh):
            vt[g, j] = jnp.transpose(kv[j, kvh + g].astype(F32)).astype(BF16)
            x = kv[j, g]
            for c in range(cands):
                cc, ss = tables(c * kvh + g, j)
                krot[c * kvh + g, j] = turn(x, cc, ss)
        return 0

    lax.fori_loop(0, me + 1, prepare, 0)
    for c in q_copies:
        c.wait()

    def forward(s, n):
        @pl.when((k >= s) & has_up)
        def _():
            w_up_copy(k - s, n).wait_recv()
            w_up_copy(k - s, n).start()

        @pl.when((k + s < nk) & has_down)
        def _():
            w_down_copy(k + s, n).wait_recv()
            w_down_copy(k + s, n).start()

    wide = 4
    per_c = kvh * group // wide
    c2 = DH ** (-0.5) * math.log2(math.e)

    def attn_copy(c, col):
        part = attn.at[col, pl.ds(c * tok, tok)]
        return remote(part, part, a_send.at[c], a_recv.at[c], mate)

    def candidate(c, _):
        def unit(i, _):
            g = i // (group // wide)
            cg = c * kvh + g
            h0 = wide * i
            cc, ss = tables(cg, me)
            qr = [turn(qv[h0 + d], cc, ss) for d in range(wide)]

            def step(j, state):
                kt = krot[cg, j]
                vv = vt[g, j]
                bj = bias[j]
                new = []
                sts = [lax.dot_general(kt, qr[d], (((1,), (1,)), ((), ())),
                                       preferred_element_type=F32) + bj
                       for d in range(wide)]
                for d in range(wide):
                    m, l, acc = state[d]
                    st = sts[d]
                    mn = jnp.maximum(m, jnp.max(st, axis=0, keepdims=True))
                    p = jnp.exp2((st - mn) * c2)
                    al = jnp.exp2((m - mn) * c2)
                    l = l * al + jnp.sum(p, axis=0, keepdims=True)
                    acc = acc * al + jnp.dot(vv, p.astype(BF16), preferred_element_type=F32)
                    new.append((mn, l, acc))
                return tuple(new)

            one = (jnp.full((1, tok), LOW, F32), jnp.zeros((1, tok), F32),
                   jnp.zeros((DH, tok), F32))
            state = lax.fori_loop(0, me + 1, step, (one,) * wide)
            for d in range(wide):
                m, l, acc = state[d]
                at = pl.multiple_of((h0 + d) * DH, DH)
                attn[y, pl.ds(pl.multiple_of(c * tok, tok), tok), pl.ds(at, DH)] = (
                    jnp.transpose(acc / l).astype(BF16))
            return 0

        lax.fori_loop(0, per_c, unit, 0)
        attn_copy(c, y).start()
        return 0

    lax.fori_loop(0, cands, candidate, 0)
    for c in w_copies:
        c.wait()
    for c in range(cands):
        attn_copy(c, other).wait_recv()

    def slot(j):
        return jnp.minimum(j - (j > t).astype(jnp.int32), nk - 2)

    def p_copy(j, n):
        return remote(pbuf.at[slot(j), n], rbuf.at[t, n], p_send.at[j, n], p_recv.at[t, n], (me, j))

    def p_arrive(src, n):
        return remote(rbuf.at[src, n], rbuf.at[src, n], p_send.at[src, n], p_recv.at[src, n],
                      (me, src))

    def y_copy(n, col):
        return remote(ybuf.at[n], obuf.at[col, n], y_send.at[n], y_recv.at[n], mate)

    def o_copy(col, n):
        return pltpu.make_async_copy(
            obuf.at[col, n],
            out_hbm.at[:, pl.ds(pl.multiple_of((col * NC + n) * cw, cw), cw)],
            o_sem.at[col, n])

    def project(j, n, dest):
        def block(half, _):
            dest[half] = jnp.dot(
                attn[half], wbuf[j, n], preferred_element_type=F32).astype(BF16)
            return 0
        lax.fori_loop(0, 2, block, 0)

    def compute(p, d, n):
        j = k - p if d == 0 else k + p
        ok = k >= p if d == 0 else k + p < nk
        fwd = has_up if d == 0 else has_down
        if p > 0:
            @pl.when(ok & jnp.logical_not(fwd))
            def _():
                (w_up_copy if d == 0 else w_down_copy)(j, n).wait_recv()
        @pl.when(ok & (j != t))
        def _():
            project(j, n, pbuf.at[slot(j), n])
            p_copy(j, n).start()

        @pl.when(ok & (j == t))
        def _():
            project(j, n, rbuf.at[t, n])

    def finish(n):
        for d in range(1, ntp):
            p_arrive(lax.rem(t + d, ntp), n).wait_recv()

        def total(half, r):
            acc = rbuf[0, n, half, pl.ds(r, BLK)].astype(F32)
            for src in range(1, ntp):
                acc = acc + rbuf[src, n, half, pl.ds(r, BLK)].astype(F32)
            return acc.astype(BF16)

        def block(b, _):
            r = pl.multiple_of(b * BLK, BLK)
            ybuf[n, pl.ds(r, BLK)] = total(other, r)
            return 0

        lax.fori_loop(0, rows // BLK, block, 0)
        y_copy(n, y).start()

        def block2(b, _):
            r = pl.multiple_of(b * BLK, BLK)
            obuf[y, n, pl.ds(r, BLK)] = total(y, r)
            return 0

        lax.fori_loop(0, rows // BLK, block2, 0)
        o_copy(y, n).start()

    for p in range(nk):
        mine = (t == k - p) | (t == k + p)

        if 0 < p < nk - 1:
            def pass_on(n, _):
                forward(p, n)
                return 0
            lax.fori_loop(0, NC, pass_on, 0)

        def chunk(n, _):
            compute(p, 0, n)
            if p > 0:
                compute(p, 1, n)

            @pl.when(mine & (n > 0))
            def _():
                finish(n - 1)
            return 0

        lax.fori_loop(0, NC, chunk, 0)

        @pl.when(mine)
        def _():
            finish(NC - 1)

    def drain(n, _):
        y_copy(n, other).wait_recv()
        o_copy(other, n).start()
        return 0

    lax.fori_loop(0, NC, drain, 0)

    def drain2(n, _):
        def sent(j, _):
            @pl.when(j != t)
            def _():
                p_copy(j, n).wait_send()
            return 0
        lax.fori_loop(0, nk, sent, 0)
        y_copy(n, y).wait_send()
        o_copy(y, n).wait()
        o_copy(other, n).wait()
        return 0

    lax.fori_loop(0, NC, drain2, 0)
    for c in range(cands):
        attn_copy(c, y).wait_send()

    def drain_kv(j, _):
        @pl.when(has_up)
        def _():
            kv_up_copy(j).wait_send()

            def each(n, _):
                w_up_copy(j, n).wait_send()
                return 0
            lax.fori_loop(0, NC, each, 0)
        kv_mate_copy(j, y).wait_send()
        return 0

    lax.fori_loop(0, k + 1, drain_kv, 0)

    @pl.when(has_down)
    def _():
        def drain_down(j, _):
            def each(n, _):
                w_down_copy(j, n).wait_send()
                return 0
            lax.fori_loop(0, NC, each, 0)
            return 0
        lax.fori_loop(k, nk, drain_down, 0)


ISSUE = (
    (0, 0, 0, 0),
    (1, 1, 1, 1),
    (0, 0, 0, 0),
    (0, 0, 0, 0),
)
LAG = 8
ORDER = (
    ((0, 0, 0, 0), (0, 1, 0, 0), (0, 2, 0, 0), (0, 3, 0, 0), (0, 0, 1, 0), (0, 1, 1, 0), (0, 2, 1, 0), (0, 3, 1, 0), (0, 0, 2, 0), (0, 1, 2, 0), (0, 2, 2, 0), (0, 3, 2, 0)),
    ((1, 0, 0, 0), (0, 0, 0, 1), (1, 0, 1, 0), (0, 1, 0, 1), (1, 0, 2, 0), (0, 2, 0, 1), (1, 0, 0, 1), (0, 3, 0, 1)),
    ((1, 1, 0, 0), (1, 1, 1, 0), (1, 1, 2, 0), (1, 1, 0, 1)),
    ((1, 0, 1, 1), (0, 0, 1, 1), (1, 1, 1, 1), (0, 1, 1, 1), (0, 2, 1, 1), (0, 3, 1, 1)),
    ((1, 2, 0, 0), (1, 2, 1, 0), (1, 2, 2, 0), (1, 2, 0, 1), (1, 2, 1, 1)),
    ((1, 3, 0, 0), (1, 3, 1, 0), (1, 3, 2, 0), (1, 3, 0, 1), (1, 3, 1, 1)),
    ((0, 0, 2, 1), (1, 0, 2, 1), (0, 1, 2, 1), (1, 1, 2, 1), (0, 2, 2, 1), (1, 2, 2, 1),
     (0, 3, 2, 1), (1, 3, 2, 1)),
)
NEEDS = ((), ((0,), (0,), False), ((), (1,), False), ((1,), (), True),
         ((), (2,), False), ((), (3,), False), ((2,), (), True))


def quad_fits(nctx, ntp, cands, cols):
    return nctx == 8 and ntp == 4 and cands == 3 and cols % (NC * DH) == 0


def quad_kernel(cands, kvh, group, tok,
                q_hbm, k_hbm, v_hbm, w_hbm, keep_ref, basec, bases, offc, offs,
                out_hbm,
                qv, kv, krot, vt, bias, attn, wbuf, give, kept, got, xgot,
                q_sem, kv_sem, kv_up, kv_y, kv_near, kv_recv, w_local, w_send, w_recv,
                a_send, a_recv, g_send, g_recv, x_send, x_recv, o_send, o_recv):
    nz = 4
    me = lax.axis_index("ctx")
    t = lax.axis_index("tp")
    z, y = me // 2, me % 2
    zh, zl = z // 2, z % 2
    x, core = t // 2, t % 2
    cw = wbuf.shape[3]
    heads = kvh * group
    half = 2 * tok
    width = group * DH
    has_up = z + 1 < nz
    has_down = z > 0
    one = jnp.int32(1)

    mate = (z * 2 + 1 - y, t)
    up = (jnp.minimum(z + 1, nz - 1) * 2 + y, t)
    down = (jnp.maximum(z - 1, 0) * 2 + y, t)
    near = ((zh * 2 + 1 - zl) * 2 + y, t)
    far = (((1 - zh) * 2 + zl) * 2 + y, t)
    sibling = (me, x * 2 + 1 - core)
    across = (me, (1 - x) * 2 + core)
    at_home = (zl == core) & (core == y)

    def remote(src, dst, ssem, rsem, dev):
        return pltpu.make_async_remote_copy(
            src_ref=src, dst_ref=dst, send_sem=ssem, recv_sem=rsem,
            device_id=dev, device_id_type=MESH)

    q_local = pltpu.make_async_copy(q_hbm, qv.at[zl], q_sem.at[0])
    q_near = remote(q_hbm, qv.at[zl], q_sem.at[1], q_sem.at[2], near)
    q_from = remote(q_hbm, qv.at[1 - zl], q_sem.at[1], q_sem.at[2], near)
    kv_copies = [
        pltpu.make_async_copy(src.at[:, pl.ds(g * DH, DH)], kv.at[me, i * kvh + g],
                              kv_sem.at[i * kvh + g])
        for i, src in enumerate((k_hbm, v_hbm)) for g in range(kvh)
    ]
    w_copies = [
        pltpu.make_async_copy(w_hbm.at[:, pl.ds(n * cw, cw)], wbuf.at[0, n], w_local.at[n])
        for n in range(NC)
    ]
    for c in kv_copies + [q_local]:
        c.start()

    def out_target(zt):
        return ((zh * 2 + zt) * 2 + core, x * 2 + zl)

    def out_source(col):
        return ((zh * 2 + core) * 2 + col, x * 2 + y)

    bar = pltpu.get_barrier_semaphore()
    for dev in (mate, near, far, sibling, across):
        pl.semaphore_signal(bar, inc=1, device_id=dev, device_id_type=MESH)

    @pl.when(has_down)
    def _():
        pl.semaphore_signal(bar, inc=1, device_id=down, device_id_type=MESH)

    for col in range(2):
        @pl.when(jnp.logical_not(at_home & (col == y)))
        def _():
            pl.semaphore_signal(bar, inc=1, device_id=out_source(col), device_id_type=MESH)

    pl.semaphore_wait(bar, 7 + has_up.astype(jnp.int32) - at_home.astype(jnp.int32))

    def kv_up_copy(j):
        s = 2 * j + y
        return remote(kv.at[s], kv.at[s], kv_up.at[j], kv_recv.at[s], up)

    def kv_mate_copy(j, col):
        s = 2 * j + col
        return remote(kv.at[s], kv.at[s], kv_y.at[j], kv_recv.at[s], mate)

    def kv_pass(j):
        @pl.when(has_up)
        def _():
            kv_up_copy(j).start()
        kv_mate_copy(j, y).start()

    def kv_near_copy(zz):
        s = 2 * zz + y
        return remote(kv.at[s], kv.at[s], kv_near.at[0], kv_recv.at[s], near)

    def w_copy(n):
        return remote(w_hbm.at[:, pl.ds(n * cw, cw)], wbuf.at[1, n],
                      w_send.at[n], w_recv.at[n], far)

    def issue(point):
        for zz in range(nz):
            for n in range(NC):
                if ISSUE[zz][n] in (point if isinstance(point, range) else (point,)):
                    here = z == zz

                    @pl.when(here)
                    def _():
                        w_copy(n).start()

    for c in kv_copies:
        c.wait()
    kv_pass(z)

    @pl.when(zl == 1)
    def _():
        kv_near_copy(z).start()
        q_near.start()

    @pl.when(z == 0)
    def _():
        q_near.start()

    issue(0)
    for c in w_copies:
        c.start()

    top = (zh * 2 + 1) * 2 + y
    blocks = bias.shape[1]
    kio = lax.broadcasted_iota(jnp.int32, (tok, tok), 0)
    qio = lax.broadcasted_iota(jnp.int32, (tok, tok), 1)
    nb = tok // BLK

    def make_bias(i, _):
        zt, j = i // blocks, i % blocks
        mine = (zh * 2 + zt) * 2 + y
        seen = jnp.zeros((tok, tok), jnp.int32)
        for a in range(nb):
            for b in range(nb):
                here = (qio // BLK == a) & (kio // BLK == b)
                seen = jnp.where(here, keep_ref[mine * nb + a, j * nb + b], seen)
        ok = (seen == 1) & (kio + (j - mine) * tok <= qio)
        bias[zt, j] = jnp.where(ok, 0.0, LOW)
        return 0

    def tables(cg, j):
        bc, bs = basec[cg], bases[cg]
        oc = offc[cg, pl.ds(j, 1)]
        os = offs[cg, pl.ds(j, 1)]
        return bc * oc - bs * os, bs * oc + bc * os

    def turn(v, c, s):
        v = v.astype(F32)
        return (v * c + pltpu.roll(v, DH // 2, 1) * s).astype(BF16)

    def prepare(zz):
        kv_mate_copy(zz, 1 - y).wait_recv()

        def block(j, _):
            for g in range(kvh):
                vt[g, j] = jnp.transpose(kv[j, kvh + g].astype(F32)).astype(BF16)
                v = kv[j, g]
                for c in range(cands):
                    cc, ss = tables(c * kvh + g, j)
                    krot[c * kvh + g, j] = turn(v, cc, ss)
            return 0

        lax.fori_loop(2 * zz, 2 * zz + 2, block, 0)

    lax.fori_loop(0, 2 * blocks, make_bias, 0)

    def fetch(s, _):
        kv_up_copy(z - s).wait_recv()
        kv_pass(z - s)
        prepare(z - s + 1)
        return 0

    lax.fori_loop(1, z + 1, fetch, 0)

    @pl.when(zl == 0)
    def _():
        @pl.when(z > 0)
        def _():
            q_near.start()
        kv_near_copy(z + 1).wait_recv()
        kv_mate_copy(z + 1, y).start()

    issue(1)
    prepare(jnp.int32(0))

    @pl.when(zl == 0)
    def _():
        prepare(z + 1)

    q_local.wait()
    q_from.wait_recv()

    pieces = cands * kvh
    c2 = DH ** (-0.5) * math.log2(math.e)

    def a_copy(i, ty, zt):
        c, g = i // kvh, i % kvh
        p = attn.at[c, pl.ds(pl.multiple_of((ty * 2 + zt) * tok, tok), tok),
                    pl.ds(pl.multiple_of(g * width, width), width)]
        return remote(p, p, a_send.at[zt, i], a_recv.at[zt, i], mate)

    def attend(i, zt):
        c, g = i // kvh, i % kvh
        mine = (zh * 2 + zt) * 2 + y
        cc, ss = tables(i, mine)
        qr = [turn(qv[zt, :, pl.ds(pl.multiple_of((g * group + d) * DH, DH), DH)], cc, ss)
              for d in range(group)]

        def step(j, state):
            js = [2 * j, jnp.minimum(2 * j + 1, top)]
            bs = [bias[zt, 2 * j], bias[zt, 2 * j + 1]]
            new = []
            sts = [[lax.dot_general(krot[i, jj], qr[d], (((1,), (1,)), ((), ())),
                                    preferred_element_type=F32) + bj
                    for jj, bj in zip(js, bs)] for d in range(group)]
            for d in range(group):
                m, l, acc = state[d]
                mn = m
                for st in sts[d]:
                    mn = jnp.maximum(mn, jnp.max(st, axis=0, keepdims=True))
                al = jnp.exp2((m - mn) * c2)
                l, acc = l * al, acc * al
                for jj, st in zip(js, sts[d]):
                    p = jnp.exp2((st - mn) * c2)
                    l = l + jnp.sum(p, axis=0, keepdims=True)
                    acc = acc + jnp.dot(vt[g, jj], p.astype(BF16), preferred_element_type=F32)
                new.append((mn, l, acc))
            return tuple(new)

        first = (jnp.full((1, tok), LOW, F32), jnp.zeros((1, tok), F32),
                 jnp.zeros((DH, tok), F32))
        state = lax.fori_loop(0, mine // 2 + 1, step, (first,) * group)
        for d in range(group):
            m, l, acc = state[d]
            at = pl.multiple_of((g * group + d) * DH, DH)
            attn[c, pl.ds(pl.multiple_of((y * 2 + zt) * tok, tok), tok), pl.ds(at, DH)] = (
                jnp.transpose(acc / l).astype(BF16))

    def piece(i, _):
        def both(k, _):
            zt = zl + k * (1 - 2 * zl)
            attend(i, zt)
            a_copy(i, y, zt).start()
            return 0

        lax.fori_loop(0, 2, both, 0)
        for zz in range(nz):
            for n in range(NC):
                if 2 <= ISSUE[zz][n] < 2 + pieces:
                    @pl.when((z == zz) & (i == ISSUE[zz][n] - 2))
                    def _():
                        w_copy(n).start()
        return 0


    def need_attn(c):
        for g in range(kvh):
            for zt in range(2):
                a_copy(c * kvh + g, 1 - y, zt).wait_recv()

    table = [v for seg in ORDER for v in seg]

    def unit_of(u):
        block = u // 12
        sh = 2 * (u % 12)

        def pick(k):
            word = jnp.int32(0)
            for b in range(0, len(table), 12):
                bits = sum(v[k] << (2 * i) for i, v in enumerate(table[b:b + 12]))
                word = jnp.where(block == b // 12, jnp.int32(bits), word)
            return lax.shift_right_logical(word, sh) & 3

        return pick(0), pick(1), pick(2), pick(3)

    def receives(w):
        return jnp.where(w == 0, zh, 1 - zh) == x

    def g_copy(u):
        return remote(give.at[u], got.at[u], g_send.at[u], g_recv.at[u], sibling)

    def x_copy(u, n, c):
        i = n * cands + c
        return remote(kept.at[u], xgot.at[i], x_send.at[i], x_recv.at[i], across)

    def o_ref(n, c, col):
        return out_hbm.at[pl.ds(pl.multiple_of(c * tok, tok), tok),
                          pl.ds(pl.multiple_of((col * NC + n) * cw, cw), cw)]

    def o_copy(u, n, c, zt):
        return remote(kept.at[u, pl.ds(zt * tok, tok)], o_ref(n, c, y),
                      o_send.at[zt, n * cands + c], o_recv.at[y, n * cands + c], out_target(zt))

    def o_local(u, n, c, zt):
        return pltpu.make_async_copy(kept.at[u, pl.ds(zt * tok, tok)], o_ref(n, c, y),
                                     o_send.at[zt, n * cands + c])

    def slot(w, n, c):
        return (w * NC + n) * cands + c

    def reduces(h):
        return (h == 0) == (core == y)

    def multiply(u):
        w, n, c, h = unit_of(u)
        i = slot(w, n, c)
        r = pl.multiple_of(jnp.where(h == 0, y, 1 - y) * half, half)
        p = jnp.dot(attn[c, pl.ds(r, half)], wbuf[w, n], preferred_element_type=F32).astype(BF16)

        @pl.when(reduces(h))
        def _():
            kept[i] = p

        @pl.when(jnp.logical_not(reduces(h)))
        def _():
            give[i] = p
            g_copy(i).start()

    def pair(u):
        w, n, c, h = unit_of(u)
        i = slot(w, n, c)

        @pl.when(reduces(h) & jnp.logical_not(receives(w)))
        def _():
            g_copy(i).wait_recv()

            def block(b, _):
                r = pl.ds(pl.multiple_of(b * BLK, BLK), BLK)
                kept[i, r] = (kept[i, r].astype(F32) + got[i, r].astype(F32)).astype(BF16)
                return 0

            lax.fori_loop(0, half // BLK, block, 0)
            x_copy(i, n, c).start()

    def finish(u):
        w, n, c, h = unit_of(u)
        i = slot(w, n, c)

        @pl.when(reduces(h) & receives(w))
        def _():
            g_copy(i).wait_recv()
            x_copy(i, n, c).wait_recv()

            def block(b, _):
                r = pl.ds(pl.multiple_of(b * BLK, BLK), BLK)
                kept[i, r] = (kept[i, r].astype(F32) + got[i, r].astype(F32)
                              + xgot[n * cands + c, r].astype(F32)).astype(BF16)
                return 0

            lax.fori_loop(0, half // BLK, block, 0)
            for zt in range(2):
                own = at_home & (zl == zt)

                @pl.when(own)
                def _():
                    o_local(i, n, c, zt).start()

                @pl.when(jnp.logical_not(own))
                def _():
                    o_copy(i, n, c, zt).start()

    for c in w_copies:
        c.wait()

    def candidate(c, _):
        lax.fori_loop(c * kvh, (c + 1) * kvh, piece, 0)

        def own(u, _):
            multiply(u)

            @pl.when(u > NC * c)
            def _():
                pair(u - 1)
            return 0

        def old(u, _):
            finish(u)
            return 0

        lax.fori_loop(NC * c, NC * (c + 1), own, 0)
        pair(NC * (c + 1) - 1)
        lax.fori_loop(NC * jnp.maximum(c - 1, 0), NC * c, old, 0)
        return 0

    lax.fori_loop(0, cands, candidate, 0)
    issue(2 + pieces)
    done = NC * (cands - 1)

    def stretch(lo, hi, lag, flush):
        nonlocal done

        def step(u, _):
            multiply(u)

            @pl.when(u > lo)
            def _():
                pair(u - 1)

            @pl.when(u - lag >= done)
            def _():
                finish(u - lag)
            return 0

        def rest(u, _):
            finish(u)
            return 0

        lax.fori_loop(lo, hi, step, 0)
        pair(jnp.int32(hi - 1))
        done = max(done, hi - lag)
        if flush:
            lax.fori_loop(done, hi, rest, 0)
            done = hi

    def need_w(n):
        w_copy(n).wait_recv()

    marks = [0]
    for seg in ORDER:
        marks.append(marks[-1] + len(seg))
    for seg, (attn_of, w_of, flush) in enumerate(NEEDS[1:], 1):
        for c in attn_of:
            need_attn(c)
        for n in w_of:
            need_w(n)
        stretch(marks[seg], marks[seg + 1], LAG, flush)
        issue(3 + pieces + seg)

    def arrived(i, _):
        n, c = i // cands, i % cands
        for col in range(2):
            @pl.when(jnp.logical_not(at_home & (col == y)))
            def _():
                remote(o_ref(n, c, col), o_ref(n, c, col), o_send.at[0, i], o_recv.at[col, i],
                       out_source(col)).wait_recv()
        return 0

    lax.fori_loop(0, NC * cands, arrived, 0)

    def drain(u, _):
        w, n, c = u // (NC * cands), (u // cands) % NC, u % cands
        g_copy(u).wait_send()

        @pl.when(receives(w))
        def _():
            for zt in range(2):
                own = at_home & (zl == zt)

                @pl.when(own)
                def _():
                    o_local(u, n, c, zt).wait()

                @pl.when(jnp.logical_not(own))
                def _():
                    o_copy(u, n, c, zt).wait_send()

        @pl.when(jnp.logical_not(receives(w)))
        def _():
            x_copy(u, n, c).wait_send()
        return 0

    lax.fori_loop(0, 2 * NC * cands, drain, 0)

    def drain_attn(i, _):
        for zt in range(2):
            a_copy(i, y, zt).wait_send()
        return 0

    lax.fori_loop(0, pieces, drain_attn, 0)
    for n in range(NC):
        w_copy(n).wait_send()

    q_near.wait_send()

    @pl.when(zl == 1)
    def _():
        kv_near_copy(z).wait_send()

    @pl.when(zl == 0)
    def _():
        kv_mate_copy(z + 1, y).wait_send()

    def drain_kv(j, _):
        @pl.when(has_up)
        def _():
            kv_up_copy(j).wait_send()
        kv_mate_copy(j, y).wait_send()
        return 0

    lax.fori_loop(0, z + 1, drain_kv, 0)


def quad(nctx, ntp, cands, kvh, group, tok, rw, cols,
         queries, keys, values, out_weight, block_keep, basec, bases, offc, offs):
    heads = kvh * group
    cg = cands * kvh
    cw = cols // NC
    units = 2 * NC * cands
    hbm = pl.BlockSpec(memory_space=pl.ANY)
    vmem = pl.BlockSpec(memory_space=pltpu.VMEM)
    dma = pltpu.SemaphoreType.DMA
    return pl.pallas_call(
        functools.partial(quad_kernel, cands, kvh, group, tok),
        out_shape=jax.ShapeDtypeStruct((cands * tok, 2 * cols), BF16),
        in_specs=[hbm] * 4 + [pl.BlockSpec(memory_space=pltpu.SMEM)] + [vmem] * 4,
        out_specs=hbm,
        scratch_shapes=[
            pltpu.VMEM((2, tok, heads * DH), BF16),
            pltpu.VMEM((nctx, 2 * kvh, tok, DH), BF16),
            pltpu.VMEM((cg, nctx, tok, DH), BF16),
            pltpu.VMEM((kvh, nctx, DH, tok), BF16),
            pltpu.VMEM((2, nctx, tok, tok), F32),
            pltpu.VMEM((cands, 4 * tok, rw), BF16),
            pltpu.VMEM((2, NC, rw, cw), BF16),
            pltpu.VMEM((units, 2 * tok, cw), BF16),
            pltpu.VMEM((units, 2 * tok, cw), BF16),
            pltpu.VMEM((units, 2 * tok, cw), BF16),
            pltpu.VMEM((NC * cands, 2 * tok, cw), BF16),
            dma((3,)), dma((2 * kvh,)), dma((nctx // 2,)), dma((nctx // 2,)), dma((1,)), dma((nctx,)),
            dma((NC,)), dma((NC,)), dma((NC,)),
            dma((2, cg)), dma((2, cg)), dma((units,)), dma((units,)),
            dma((NC * cands,)), dma((NC * cands,)), dma((2, NC * cands)), dma((2, NC * cands)),
        ],
        compiler_params=pltpu.CompilerParams(
            collective_id=0, has_side_effects=True, vmem_limit_bytes=63 * 2**20),
        cost_estimate=pl.CostEstimate(
            flops=4 * nctx * tok * tok * heads * cands * DH + 4 * 4 * cands * tok * rw * cols,
            bytes_accessed=4 * rw * cols * 2,
            transcendentals=nctx * tok * tok * heads * cands),
        name="attend_project",
    )(queries, keys, values, out_weight, block_keep, basec, bases, offc, offs)


def body(nctx, ntp, queries, keys, values, block_keep, scale_pick, scale_table, out_weight):
    tok = queries.shape[0]
    kvh = keys.shape[1] // DH
    group = queries.shape[1] // (kvh * DH)
    cands = scale_pick.shape[0]
    kv_all = scale_pick.shape[1]
    table_rows = scale_table.shape[0]
    rw, cols = out_weight.shape
    nk = nctx // 2
    cw = cols // NC
    heads = kvh * group
    rows = cands * tok
    here = lax.axis_index("tp") * kvh + jnp.arange(kvh, dtype=jnp.int32)
    select = jnp.arange(kv_all, dtype=jnp.int32)[None, :] == here[:, None]
    picks = jnp.sum(jnp.where(select[None], scale_pick[:, None, :], 0), axis=-1)
    hit = picks[..., None] == jnp.arange(table_rows, dtype=jnp.int32)
    scales = jnp.sum(jnp.where(hit[..., None], scale_table[None, None], 0.0), axis=2)
    inv = 1.0 / THETA ** (jnp.arange(DH // 2, dtype=F32) * 2.0 / DH)
    freq = (inv / scales).reshape(cands * kvh, 1, DH // 2)

    def table(positions):
        angle = positions.astype(F32)[None, :, None] * freq
        c, s = jnp.cos(angle), jnp.sin(angle)
        return jnp.concatenate([c, c], -1), jnp.concatenate([-s, s], -1)

    basec, bases = table(jnp.arange(tok, dtype=jnp.int32))
    offc, offs = table(jnp.arange(nctx, dtype=jnp.int32) * tok)
    cg = cands * kvh
    hbm = pl.BlockSpec(memory_space=pl.ANY)
    vmem = pl.BlockSpec(memory_space=pltpu.VMEM)
    dma = pltpu.SemaphoreType.DMA
    if quad_fits(nctx, ntp, cands, cols):
        out = quad(nctx, ntp, cands, kvh, group, tok, rw, cols,
                   queries, keys, values, out_weight, block_keep, basec, bases, offc, offs)
        return out.reshape(cands, tok, 2 * cols)
    flops = 4 * nctx * tok * tok * heads * cands * DH + 4 * rows * rw * cols * nk
    out = pl.pallas_call(
        functools.partial(chain_kernel, nctx, ntp, cands, kvh, group, tok),
        out_shape=jax.ShapeDtypeStruct((rows, 2 * cols), BF16),
        in_specs=[hbm] * 4 + [pl.BlockSpec(memory_space=pltpu.SMEM)] + [vmem] * 4,
        out_specs=hbm,
        scratch_shapes=[
            pltpu.VMEM((heads, tok, DH), BF16),
            pltpu.VMEM((nctx, 2 * kvh, tok, DH), BF16),
            pltpu.VMEM((cg, nctx, tok, DH), BF16),
            pltpu.VMEM((kvh, nctx, DH, tok), BF16),
            pltpu.VMEM((nctx, tok, tok), F32),
            pltpu.VMEM((2, rows, rw), BF16),
            pltpu.VMEM((nk, NC, rw, cw), BF16),
            pltpu.VMEM((nk - 1, NC, 2, rows, cw), BF16),
            pltpu.VMEM((ntp, NC, 2, rows, cw), BF16),
            pltpu.VMEM((2, NC, rows, cw), BF16),
            pltpu.VMEM((NC, rows, cw), BF16),
            dma((heads,)), dma((2 * kvh,)), dma((nk,)), dma((nk,)), dma((nctx,)),
            dma((NC,)), dma((2, nk * NC)), dma((nk * NC,)),
            dma((cands,)), dma((cands,)), dma((nk, NC)), dma((ntp, NC)),
            dma((NC,)), dma((NC,)), dma((2, NC)),
        ],
        compiler_params=pltpu.CompilerParams(
            collective_id=0, has_side_effects=True, vmem_limit_bytes=63 * 2**20),
        cost_estimate=pl.CostEstimate(
            flops=flops, bytes_accessed=4 * rw * cols * nk,
            transcendentals=nctx * tok * tok * heads * cands),
        name="attend_project",
    )(queries, keys, values, out_weight, block_keep, basec, bases, offc, offs)
    return out.reshape(cands, tok, 2 * cols)


def solution(mesh):
    return jax.shard_map(
        functools.partial(body, mesh.shape["ctx"], mesh.shape["tp"]),
        mesh=mesh,
        in_specs=(P("ctx", "tp"), P("ctx", "tp"), P("ctx", "tp"), P(), P(), P(), P("tp", "ctx")),
        out_specs=P(None, "ctx", "tp"),
        check_vma=False,
    )
```
